128 devices in a mesh: row: 32 (over y, x, z_hi), col: 4 (over z_lo, core).
Axes of the slice: x: 4, y: 4, z: 4 (z_hi: 2, z_lo: 2; z = z_hi * 2 + z_lo), core: 2. Of those that a mesh axis runs over, the one named last changes fastest.
Arguments:
- front_inverse: bfloat16 [24576, 24576], P('row', 'col'), may hold values from -0.0390625 to 0.0390625
- coupling_tiles: bfloat16 [768, 128, 128], P('col'), may hold values from -12 to 12
- tile_row: int32 [768], P('col'), may hold values from 0 to 191, as said below
- tile_col: int32 [768], P('col'), may hold values from 0 to 15
- surface_map: int32 [2, 8192], P(None, 'row'), may hold values from 0 to 24575, as said below
- bem_entries: bfloat16 [2, 8192, 2048], P(None, 'row', 'col'), may hold values from -6 to 6
- pivot_inverse: bfloat16 [8192, 8192], P('row'), may hold values from -0.0625 to 0.0625
- slab_below: bfloat16 [8192, 8192], P('row'), may hold values from -0.0625 to 0.0625
Outputs:
- panel_out: bfloat16 [2, 8192, 2048], P(None, 'row', 'col')
The draws below stay inside these ranges and needn't reach their ends.
Inputs may be any that keep to these rules, and one draw needn't show every extreme that they name: `tile_row`: tiles at positions c * 192 to (c + 1) * 192 - 1 lie in block rows c * 48 to (c + 1) * 48 - 1; no two tiles share both block row and block column. `surface_map`: all entries differ; of the entries in the columns of one index of row, at most 24 lie in any one block of 768 front rows that starts at a multiple of 768, and for every index of row some block holds exactly 24 of them.
All inputs are finite; a program needn't handle non-finite values.
Results may differ from the reference program's by a relative error of at most 0.0058.
Values may be sent and summed in bfloat16 or wider, within the bound.
A program may use at most 192 MiB of HBM per device.

```python
import jax
import jax.numpy as jnp

NF = 24576
KS = 8192
COLS = 2048
BR_COL = 48
TILES_COL = 192
ROUTE_CAP = 24
N_ROW = 32
N_COL = 4


def tile_pairs(key):
    base_key = jax.random.fold_in(key, 7)
    col_blocks = COLS // 128
    slot_total = BR_COL * col_blocks
    shards = NF // (128 * BR_COL)

    def shard_draw(shard):
        picked = jax.random.permutation(jax.random.fold_in(base_key, shard), slot_total)[:TILES_COL]
        return (shard * BR_COL + picked // col_blocks, picked % col_blocks)
    block_rows, block_cols = jax.vmap(shard_draw)(jnp.arange(shards, dtype=jnp.int32))
    return (block_rows.reshape(-1).astype(jnp.int32), block_cols.reshape(-1).astype(jnp.int32))


def draw_tile_row(key, part):
    return tile_pairs(key)[0]


def draw_tile_col(key, part):
    return tile_pairs(key)[1]


def draw_surface_map(key, part):
    base_key = jax.random.fold_in(key, 11)
    row_width = NF // N_ROW
    per_device = 2 * (KS // N_ROW)
    capacity = ROUTE_CAP
    shuffle_key = jax.random.fold_in(base_key, 1)
    shuffles = jax.vmap(lambda owner: jax.random.permutation(jax.random.fold_in(shuffle_key, owner), row_width))(jnp.arange(N_ROW, dtype=jnp.int32))

    def device_draw(device):
        device_key = jax.random.fold_in(jax.random.fold_in(base_key, 2), device)
        owner_order = jax.random.permutation(jax.random.fold_in(device_key, 0), N_ROW)
        entry = jnp.arange(per_device, dtype=jnp.int32)
        later = jnp.maximum(entry - capacity, 0)
        spot = jnp.where(entry < capacity, 0, 1 + later % (N_ROW - 1))
        within = jnp.where(entry < capacity, entry, later // (N_ROW - 1))
        owners = owner_order[spot]
        front_rows = owners * row_width + shuffles[owners, device * capacity + within]
        order = jax.random.permutation(jax.random.fold_in(device_key, 1), per_device)
        return front_rows[order]
    every = jax.vmap(device_draw)(jnp.arange(N_ROW, dtype=jnp.int32))
    every = every.reshape(N_ROW, 2, KS // N_ROW).transpose(1, 0, 2).reshape(2, KS)
    return every.astype(jnp.int32)


def block_scale(rng, dims, cuts, least, high):
    level, own = 1.0, jax.random.fold_in(rng, 6)
    for dim, parts in cuts:
        heights = jnp.exp(jax.random.uniform(jax.random.fold_in(own, dim), (parts,), jnp.float32, least / len(cuts), high / len(cuts)))
        level = level * jnp.repeat(heights, dims[dim] // parts).reshape([-1 if axis == dim else 1 for axis in range(len(dims))])
    return level


def normal_values(stream_key, dims, spread, reach, pieces=(), kind=jnp.bfloat16):
    drawn = jax.random.normal(stream_key, dims, jnp.float32) * spread
    if len(pieces) > 0:
        drawn = block_scale(stream_key, dims, pieces, -0.22, 0.18) * drawn
    return jnp.clip(drawn, min=-reach, max=reach).astype(kind)


def setup_inputs(seed: int = 0) -> dict:
    key_of = jax.random.split(jax.random.key(seed), 9)
    return {
        "front_inverse": normal_values(key_of[0], (NF, NF), NF ** -0.5, 0.0390625, ((0, 32), (1, 4))),
        "coupling_tiles": normal_values(key_of[1], (N_COL * TILES_COL, 128, 128), 2.0, 12.0, ((0, 4),)),
        "tile_row": draw_tile_row(jax.random.fold_in(key_of[8], 71), 0),
        "tile_col": draw_tile_col(jax.random.fold_in(key_of[8], 71), 0),
        "surface_map": draw_surface_map(jax.random.fold_in(key_of[8], 71), 0),
        "bem_entries": normal_values(key_of[5], (2, KS, COLS), 1.0, 6.0, ((1, 32), (2, 4))),
        "pivot_inverse": normal_values(key_of[6], (KS, KS), KS ** -0.5, 0.0625, ((0, 32),)),
        "slab_below": normal_values(key_of[7], (KS, KS), KS ** -0.5, 0.0625, ((0, 32),)),
    }


def reference(front_inverse, coupling_tiles, tile_row, tile_col, surface_map, bem_entries, pivot_inverse, slab_below):
    col_blocks = COLS // 128
    blocks = jnp.zeros((NF // 128, col_blocks, 128, 128), jnp.bfloat16)
    blocks = blocks.at[tile_row, tile_col].set(coupling_tiles)
    coupling = blocks.transpose(0, 2, 1, 3).reshape(NF, COLS)
    selected = front_inverse[surface_map.reshape(-1)]
    schur_part = jnp.dot(selected, coupling, preferred_element_type=jnp.float32).astype(jnp.bfloat16)
    schur_part = schur_part.reshape(2, KS, COLS)
    assembled = (bem_entries.astype(jnp.float32) - schur_part.astype(jnp.float32)).astype(jnp.bfloat16)
    pivot_solved = jnp.dot(pivot_inverse, assembled[0], preferred_element_type=jnp.float32).astype(jnp.bfloat16)
    update = jnp.dot(slab_below, pivot_solved, preferred_element_type=jnp.float32)
    below = (assembled[1].astype(jnp.float32) - update).astype(jnp.bfloat16)
    return jnp.stack([pivot_solved, below])
```

```python
import functools
import heapq

import jax
import jax.numpy as jnp
from jax import lax
from jax.experimental import pallas as pl
from jax.experimental.pallas import tpu as pltpu
from jax.sharding import PartitionSpec as P

MESH = pl.DeviceIdType.MESH
F32, BF16, I32 = jnp.float32, jnp.bfloat16, jnp.int32
N_ROW, CAP = 32, 24
SLOTS = N_ROW * CAP
ROWS = 768
GROUP = 4
TILES = 192
CHUNKS = (TILES + 16 * (GROUP - 1)) // GROUP
UNROLL = 2


def front_kernel(trow, tcol, f_hbm, t_hbm, out_hbm, f, w, acc, ob, lrs, ccol, pos, cnt, fsem, tsem, osem):
    load = pltpu.make_async_copy(f_hbm, f, fsem)
    load.start()
    first = lax.axis_index("col") * 48
    chunks = w.shape[0]

    @pl.loop(0, 16)
    def _(b):
        cnt[b] = 0

    @pl.loop(0, TILES)
    def _(i):
        b = tcol[i]
        cnt[b] = cnt[b] + 1

    def place(b, at):
        n = cnt[b]
        used = (n + GROUP - 1) // GROUP
        pos[b] = at * GROUP

        def name(c, _):
            ccol[at + c] = b
            return 0

        lax.fori_loop(0, used, name, 0)

        def clear(s, _):
            lrs[s] = 0
            w[s // GROUP, pl.ds(pl.multiple_of((s % GROUP) * 128, 128), 128), :] = jnp.zeros((128, 128), BF16)
            return 0

        lax.fori_loop(at * GROUP + n, (at + used) * GROUP, clear, 0)
        return at + used

    total = lax.fori_loop(0, 16, place, 0)

    @pl.loop(0, TILES)
    def _(i):
        b = tcol[i]
        s = pos[b]
        pos[b] = s + 1
        lrs[s] = trow[i] - first
        pltpu.make_async_copy(
            t_hbm.at[i], w.at[s // GROUP, pl.ds(pl.multiple_of((s % GROUP) * 128, 128), 128), :], tsem
        ).start()

    acc[...] = jnp.zeros_like(acc)

    @pl.when(total % UNROLL != 0)
    def _():
        ccol[total] = 0
        for g in range(GROUP):
            lrs[total * GROUP + g] = 0
        w[total] = jnp.zeros((GROUP * 128, 128), BF16)

    @pl.loop(0, TILES)
    def _(i):
        pltpu.make_async_copy(t_hbm.at[0], w.at[0, pl.ds(0, 128), :], tsem).wait()

    load.wait()

    @pl.loop(0, (total + UNROLL - 1) // UNROLL)
    def _(it):
        for u in range(UNROLL):
            c = it * UNROLL + u
            parts = []
            for g in range(GROUP):
                lr = pl.multiple_of(lrs[c * GROUP + g] * 128, 128)
                parts.append(f[:, pl.ds(lr, 128)])
            lhs = jnp.concatenate(parts, axis=1)
            at = pl.multiple_of(ccol[c] * 128, 128)
            acc[:, pl.ds(at, 128)] += jnp.dot(lhs, w[c], preferred_element_type=F32)

    for k in range(4):
        ob[k] = acc[:, k * 512 : (k + 1) * 512].astype(BF16)
        pltpu.make_async_copy(ob.at[k], out_hbm.at[k], osem.at[k]).start()
    for k in range(4):
        pltpu.make_async_copy(ob.at[k], out_hbm.at[k], osem.at[k]).wait()


def front(trow, tcol, f, tiles):
    smem = pl.BlockSpec(memory_space=pltpu.SMEM)
    hbm = pl.BlockSpec(memory_space=pl.ANY)
    chunks = CHUNKS + CHUNKS % UNROLL
    return pl.pallas_call(
        front_kernel,
        out_shape=jax.ShapeDtypeStruct((4, ROWS, 512), BF16),
        in_specs=[smem, smem, hbm, hbm],
        out_specs=hbm,
        scratch_shapes=[
            pltpu.VMEM((ROWS, 6144), BF16),
            pltpu.VMEM((chunks, GROUP * 128, 128), BF16),
            pltpu.VMEM((ROWS, 2048), F32),
            pltpu.VMEM((4, ROWS, 512), BF16),
            pltpu.SMEM((chunks * GROUP,), I32),
            pltpu.SMEM((chunks,), I32),
            pltpu.SMEM((16,), I32),
            pltpu.SMEM((16,), I32),
            pltpu.SemaphoreType.DMA,
            pltpu.SemaphoreType.DMA,
            pltpu.SemaphoreType.DMA((4,)),
        ],
        compiler_params=pltpu.CompilerParams(vmem_limit_bytes=56 << 20),
        name="front",
    )(trow, tcol, f, tiles)


def route_kernel(
    req, slotcol, part, bem, out, x, o, of, r, reqin, cv, perm, sm, rb,
    ps, pr, rs, rr, sends, recvs,
):
    me, col = lax.axis_index("row"), lax.axis_index("col")
    q, lo = col % 2, col // 2
    barrier = pltpu.get_barrier_semaphore()

    def tell(a, b):
        pl.semaphore_signal(barrier, inc=1, device_id=(a, b), device_id_type=MESH)

    tell(me, lo * 2 + 1 - q)
    tell(me, (1 - lo) * 2 + q)

    @pl.loop(1, N_ROW)
    def _(p):
        for l in range(2):
            tell(lax.rem(me + p, N_ROW), l * 2 + q)

    pl.semaphore_wait(barrier, 64)

    def swap(l):
        return pltpu.make_async_remote_copy(
            part.at[l * 2 + 1 - q], x.at[l], ps.at[l], pr.at[l], device_id=(me, lo * 2 + 1 - q), device_id_type=MESH
        )

    def ask(s, who):
        return pltpu.make_async_remote_copy(
            req.at[s], reqin.at[who], rs.at[s], rr.at[who], device_id=(s, col), device_id_type=MESH
        )

    def give(l, d, who, wl):
        return pltpu.make_async_remote_copy(
            o.at[l, d], r.at[wl, who], sends.at[l, d], recvs.at[wl, who],
            device_id=(d, l * 2 + q), device_id_type=MESH,
        )

    swap(0).start()
    swap(1).start()

    @pl.loop(1, N_ROW)
    def _(p):
        ask(lax.rem(me + p, N_ROW), me).start()

    reqin[me] = req[me]

    @pl.loop(1, N_ROW)
    def _(p):
        s = lax.rem(me + p, N_ROW)
        ask(s, s).wait_recv()

    lane = lax.broadcasted_iota(I32, (CAP, 128), 1)
    line = lax.broadcasted_iota(I32, (CAP, 128), 0)

    @pl.loop(0, N_ROW)
    def _(d):
        row = jnp.broadcast_to(reqin[d], (CAP, 128))
        val = jnp.sum(jnp.where(lane == line, row, 0), axis=1, keepdims=True)
        cv[pl.ds(pl.multiple_of(d * CAP, 8), CAP), :] = jnp.broadcast_to(val, (CAP, 128))

    @pl.loop(0, SLOTS // 128)
    def _(b):
        at = pl.ds(pl.multiple_of(b * 128, 128), 128)
        want = cv[at, :]
        for j in range(ROWS // 128):
            here = lax.broadcasted_iota(I32, (128, 128), 1) + j * 128
            perm[at, j * 128 : (j + 1) * 128] = (want == here).astype(F32).astype(BF16)

    for l in range(2):
        swap(l).wait_recv()
        sm[...] = (part[l * 2 + q].astype(F32) + x[l].astype(F32)).astype(BF16)
        of[...] = jnp.dot(perm[...], sm[...], preferred_element_type=F32)

        @pl.loop(0, N_ROW)
        def _(d):
            o[l, d] = of[pl.ds(pl.multiple_of(d * CAP, 8), CAP), :].astype(BF16)

        @pl.loop(1, N_ROW)
        def _(p):
            give(l, lax.rem(me + p, N_ROW), me, lo).start()

    give(1 - lo, me, me, lo).start()
    r[lo, me] = o[lo, me]
    give(lo, me, me, 1 - lo).wait_recv()
    of[pl.ds(pl.multiple_of(me * CAP, 8), CAP), :] = r[0, me].astype(F32) + r[1, me].astype(F32)

    @pl.loop(1, N_ROW)
    def _(p):
        s = lax.rem(me + N_ROW - p, N_ROW)
        for l in range(2):
            give(lo, s, s, l).wait_recv()
        of[pl.ds(pl.multiple_of(s * CAP, 8), CAP), :] = r[0, s].astype(F32) + r[1, s].astype(F32)

    rb[...] = of[...].astype(BF16)
    for p in range(2):
        pick = slotcol[p * 256 : (p + 1) * 256, :]
        sel = jnp.concatenate(
            [
                (pick == lax.broadcasted_iota(I32, (256, 128), 1) + j * 128).astype(F32).astype(BF16)
                for j in range(SLOTS // 128)
            ],
            axis=1,
        )
        schur = jnp.dot(sel, rb[...], preferred_element_type=F32)
        out[p] = (bem[p].astype(F32) - schur).astype(BF16)

    for l in range(2):
        swap(l).wait_send()
    give(1 - lo, me, me, lo).wait_send()

    @pl.loop(1, N_ROW)
    def _(p):
        d = lax.rem(me + p, N_ROW)
        ask(d, me).wait_send()
        for l in range(2):
            give(l, d, me, lo).wait_send()


def route(req, slotcol, part, bem):
    vm = pl.BlockSpec(memory_space=pltpu.VMEM)
    dma = pltpu.SemaphoreType.DMA
    return pl.pallas_call(
        route_kernel,
        out_shape=jax.ShapeDtypeStruct((2, 256, 512), BF16),
        in_specs=[vm] * 4,
        out_specs=vm,
        scratch_shapes=[
            pltpu.VMEM((2, ROWS, 512), BF16),
            pltpu.VMEM((2, N_ROW, CAP, 512), BF16),
            pltpu.VMEM((SLOTS, 512), F32),
            pltpu.VMEM((2, N_ROW, CAP, 512), BF16),
            pltpu.VMEM((N_ROW, 1, 128), I32),
            pltpu.VMEM((SLOTS, 128), I32),
            pltpu.VMEM((SLOTS, ROWS), BF16),
            pltpu.VMEM((ROWS, 512), BF16),
            pltpu.VMEM((SLOTS, 512), BF16),
            dma((2,)), dma((2,)), dma((N_ROW,)), dma((N_ROW,)), dma((2, N_ROW)), dma((2, N_ROW)),
        ],
        compiler_params=pltpu.CompilerParams(collective_id=0, has_side_effects=True, vmem_limit_bytes=56 << 20),
        name="route",
    )(req, slotcol, part, bem)


def plan():
    free, heap, sends, arrivals = {}, [], [], []
    count = 0

    def send(t, item, h, stage, step):
        nonlocal count
        link = ("z", 0) if stage == 0 else ((h + stage) % 2, step)
        busy = 5.6 if stage == 0 else 2.8
        go = max(t, free.get(link, 0.0))
        free[link] = go + busy
        count += 1
        heapq.heappush(heap, (go + busy + 1.5, count, item, h, stage, step))
        return (item, h, stage, step)

    def spread(t, item, h):
        k, m, z = item
        out = []
        if m == 0 and k == 0:
            out += [send(t, item, h, 1, s) for s in ((1, -1) if z == 0 else (-1, 1))]
        if m == 0:
            out += [send(t, item, h, 2, s) for s in ((1, -1) if (k + z) % 2 == 0 else (-1, 1))]
        return out

    start = []
    for h in range(2):
        start.append(send(0.0, (0, 0, 0), h, 0, 0))
    first = [spread(0.0, (0, 0, 0), h) for h in range(2)]
    for a, b in zip(*first):
        start += [a, b]
    while heap:
        t, _, (k, m, z), h, stage, step = heapq.heappop(heap)
        out = []
        if stage == 0:
            item = (0, 0, 1)
        elif stage == 1:
            item = ((k - step + 1) % 4 - 1 if k - step != -2 else 2, 0, z)
            if k == 0 and step == (1 if z == 0 else -1):
                out.append(send(t, item, h, 1, step))
        else:
            item = (k, (m - step + 1) % 4 - 1 if m - step != -2 else 2, z)
            if m == 0 and step == (1 if (k + z) % 2 == 0 else -1):
                out.append(send(t, item, h, 2, step))
        out += spread(t, item, h)
        arrivals.append((item, h, out))
    return start, arrivals


def panel_kernel(asm, a_piv, a_low, out, a0, a1, b0, b1, acc, asem, send_sem, recv_sem):
    me, col = lax.axis_index("row"), lax.axis_index("col")
    my, mx, mz = me // 8, (me // 2) % 4, me % 2

    def slot(dy, dx, dz):
        return (((my + dy + 4) % 4) * 4 + (mx + dx + 4) % 4) * 2 + (mz + dz) % 2

    loads = [pltpu.make_async_copy(a_piv, a0, asem.at[0]), pltpu.make_async_copy(a_low, a1, asem.at[1])]
    for load in loads:
        load.start()
    barrier = pltpu.get_barrier_semaphore()
    for d in ((1, 0, 0), (-1, 0, 0), (0, 1, 0), (0, -1, 0), (0, 0, 1)):
        pl.semaphore_signal(barrier, inc=1, device_id=(slot(*d), col), device_id_type=MESH)

    def at(item, h):
        k, m, z = item
        return slot(m, k, z) if h == 0 else slot(k, m, z)

    start, arrivals = plan()

    def gather(phase, a, b, load):
        sent = []

        def go(one):
            item, h, stage, step = one
            where = at(item, h)
            if stage == 0:
                to = slot(0, 0, 1)
            elif (h + stage) % 2 == 1:
                to = slot(0, step, 0)
            else:
                to = slot(step, 0, 0)
            copy = pltpu.make_async_remote_copy(
                b.at[where, h], b.at[where, h], send_sem.at[phase, len(sent)], recv_sem.at[phase, where, h],
                device_id=(to, col), device_id_type=MESH,
            )
            copy.start()
            sent.append(copy)

        def product(pair):
            cols = [a[:, pl.ds(pl.multiple_of(at(i, h) * 256 + h * 128, 128), 128)] for i, h in pair]
            rows = [b[at(i, h), h] for i, h in pair]
            return jnp.dot(jnp.concatenate(cols, axis=1), jnp.concatenate(rows, axis=0), preferred_element_type=F32)

        for one in start:
            go(one)
        load.wait()
        acc[...] = product([((0, 0, 0), 0), ((0, 0, 0), 1)])
        held = []
        for item, h, out_sends in arrivals:
            where = at(item, h)
            pltpu.make_async_remote_copy(
                b.at[where, h], b.at[where, h], send_sem.at[phase, 0], recv_sem.at[phase, where, h],
                device_id=(me, col), device_id_type=MESH,
            ).wait_recv()
            for one in out_sends:
                go(one)
            held.append((item, h))
            if len(held) == 2:
                acc[...] += product(held)
                held = []
        return sent

    b0[me, 0] = asm[0, :128, :]
    b0[me, 1] = asm[0, 128:, :]
    pl.semaphore_wait(barrier, 5)
    sent = gather(0, a0, b0, loads[0])
    solved = acc[...].astype(BF16)
    b1[me, 0] = solved[:128]
    b1[me, 1] = solved[128:]
    out[0] = solved
    sent += gather(1, a1, b1, loads[1])
    out[1] = (asm[1].astype(F32) - acc[...]).astype(BF16)
    for copy in sent:
        copy.wait_send()


def panel(asm, a_piv, a_low):
    vm = pl.BlockSpec(memory_space=pltpu.VMEM)
    hbm = pl.BlockSpec(memory_space=pl.ANY)
    dma = pltpu.SemaphoreType.DMA
    start, arrivals = plan()
    sends = len(start) + sum(len(a[2]) for a in arrivals)
    return pl.pallas_call(
        panel_kernel,
        out_shape=jax.ShapeDtypeStruct((2, 256, 512), BF16),
        in_specs=[vm, hbm, hbm],
        out_specs=vm,
        scratch_shapes=[
            pltpu.VMEM((256, 8192), BF16),
            pltpu.VMEM((256, 8192), BF16),
            pltpu.VMEM((N_ROW, 2, 128, 512), BF16),
            pltpu.VMEM((N_ROW, 2, 128, 512), BF16),
            pltpu.VMEM((256, 512), F32),
            dma((2,)), dma((2, sends)), dma((2, N_ROW, 2)),
        ],
        compiler_params=pltpu.CompilerParams(collective_id=1, has_side_effects=True, vmem_limit_bytes=56 << 20),
        name="panel",
    )(asm, a_piv, a_low)


def routes(surface_map):
    flat = surface_map.reshape(-1)
    owner, local = flat // ROWS, flat % ROWS
    n = flat.shape[0]
    ids = jnp.arange(n, dtype=I32)
    before = (owner[:, None] == owner[None, :]) & (ids[None, :] < ids[:, None])
    slot = owner * CAP + jnp.sum(before.astype(I32), axis=1)
    want = jnp.arange(N_ROW * 128, dtype=I32)
    at = jnp.where(want % 128 < CAP, (want // 128) * CAP + want % 128, -1)
    hit = at[:, None] == slot[None, :]
    req = jnp.sum(jnp.where(hit, local[None, :] + 1, 0), axis=1) - 1
    return req.reshape(N_ROW, 1, 128), jnp.broadcast_to(slot[:, None], (n, 128))


def per_device(front_inverse, tiles, tile_row, tile_col, surface_map, bem, pivot, below):
    req, slotcol = routes(surface_map)
    part = front(tile_row, tile_col, front_inverse, tiles)
    asm = route(req, slotcol, part, bem)
    return panel(asm, pivot, below)


def solution(mesh):
    placed = (
        P("row", "col"),
        P("col", None, None),
        P("col"),
        P("col"),
        P(None, "row"),
        P(None, "row", "col"),
        P("row", None),
        P("row", None),
    )
    return jax.shard_map(
        per_device, mesh=mesh, in_specs=placed, out_specs=P(None, "row", "col"), check_vma=False
    )
```

```python
import jax
import jax.numpy as jnp
from jax import lax
from jax.experimental import pallas as pl
from jax.experimental.pallas import tpu as pltpu
from jax.sharding import PartitionSpec as P

MESH = pl.DeviceIdType.MESH
F32, BF16, I32 = jnp.float32, jnp.bfloat16, jnp.int32
N_ROW, CAP = 32, 24
SLOTS = N_ROW * CAP
ROWS = 768
GROUP = 4
TILES = 192
CHUNKS = (TILES + 16 * (GROUP - 1)) // GROUP
UNROLL = 2


def front_kernel(trow, tcol, f_hbm, t_hbm, out_hbm, f, w, acc, ob, lrs, ccol, pos, cnt, fsem, tsem, osem):
    load = pltpu.make_async_copy(f_hbm, f, fsem)
    load.start()
    first = lax.axis_index("col") * 48
    chunks = w.shape[0]

    @pl.loop(0, 16)
    def _(b):
        cnt[b] = 0

    @pl.loop(0, TILES)
    def _(i):
        b = tcol[i]
        cnt[b] = cnt[b] + 1

    def place(b, at):
        n = cnt[b]
        used = (n + GROUP - 1) // GROUP
        pos[b] = at * GROUP

        def name(c, _):
            ccol[at + c] = b
            return 0

        lax.fori_loop(0, used, name, 0)

        def clear(s, _):
            lrs[s] = 0
            w[s // GROUP, pl.ds(pl.multiple_of((s % GROUP) * 128, 128), 128), :] = jnp.zeros((128, 128), BF16)
            return 0

        lax.fori_loop(at * GROUP + n, (at + used) * GROUP, clear, 0)
        return at + used

    total = lax.fori_loop(0, 16, place, 0)

    @pl.loop(0, TILES)
    def _(i):
        b = tcol[i]
        s = pos[b]
        pos[b] = s + 1
        lrs[s] = trow[i] - first
        pltpu.make_async_copy(
            t_hbm.at[i], w.at[s // GROUP, pl.ds(pl.multiple_of((s % GROUP) * 128, 128), 128), :], tsem
        ).start()

    acc[...] = jnp.zeros_like(acc)

    @pl.when(total % UNROLL != 0)
    def _():
        ccol[total] = 0
        for g in range(GROUP):
            lrs[total * GROUP + g] = 0
        w[total] = jnp.zeros((GROUP * 128, 128), BF16)

    @pl.loop(0, TILES)
    def _(i):
        pltpu.make_async_copy(t_hbm.at[0], w.at[0, pl.ds(0, 128), :], tsem).wait()

    load.wait()

    @pl.loop(0, (total + UNROLL - 1) // UNROLL)
    def _(it):
        for u in range(UNROLL):
            c = it * UNROLL + u
            parts = []
            for g in range(GROUP):
                lr = pl.multiple_of(lrs[c * GROUP + g] * 128, 128)
                parts.append(f[:, pl.ds(lr, 128)])
            lhs = jnp.concatenate(parts, axis=1)
            at = pl.multiple_of(ccol[c] * 128, 128)
            acc[:, pl.ds(at, 128)] += jnp.dot(lhs, w[c], preferred_element_type=F32)

    for k in range(4):
        ob[k] = acc[:, k * 512 : (k + 1) * 512].astype(BF16)
        pltpu.make_async_copy(ob.at[k], out_hbm.at[k], osem.at[k]).start()
    for k in range(4):
        pltpu.make_async_copy(ob.at[k], out_hbm.at[k], osem.at[k]).wait()


def front(trow, tcol, f, tiles):
    smem = pl.BlockSpec(memory_space=pltpu.SMEM)
    hbm = pl.BlockSpec(memory_space=pl.ANY)
    chunks = CHUNKS + CHUNKS % UNROLL
    return pl.pallas_call(
        front_kernel,
        out_shape=jax.ShapeDtypeStruct((4, ROWS, 512), BF16),
        in_specs=[smem, smem, hbm, hbm],
        out_specs=hbm,
        scratch_shapes=[
            pltpu.VMEM((ROWS, 6144), BF16),
            pltpu.VMEM((chunks, GROUP * 128, 128), BF16),
            pltpu.VMEM((ROWS, 2048), F32),
            pltpu.VMEM((4, ROWS, 512), BF16),
            pltpu.SMEM((chunks * GROUP,), I32),
            pltpu.SMEM((chunks,), I32),
            pltpu.SMEM((16,), I32),
            pltpu.SMEM((16,), I32),
            pltpu.SemaphoreType.DMA,
            pltpu.SemaphoreType.DMA,
            pltpu.SemaphoreType.DMA((4,)),
        ],
        compiler_params=pltpu.CompilerParams(vmem_limit_bytes=56 << 20),
        cost_estimate=pl.CostEstimate(flops=20 << 30, bytes_accessed=60 << 20, transcendentals=0),
        name="front",
    )(trow, tcol, f, tiles)


def route_kernel(
    req, slotcol, part, bem, out, x, o, of, r, reqin, cv, perm, sm, rb,
    ps, pr, rs, rr, sends, recvs,
):
    me, col = lax.axis_index("row"), lax.axis_index("col")
    q, lo = col % 2, col // 2
    barrier = pltpu.get_barrier_semaphore()

    def tell(a, b):
        pl.semaphore_signal(barrier, inc=1, device_id=(a, b), device_id_type=MESH)

    tell(me, lo * 2 + 1 - q)
    tell(me, (1 - lo) * 2 + q)

    @pl.loop(1, N_ROW)
    def _(p):
        for l in range(2):
            tell(lax.rem(me + p, N_ROW), l * 2 + q)

    pl.semaphore_wait(barrier, 64)

    def swap(l):
        return pltpu.make_async_remote_copy(
            part.at[l * 2 + 1 - q], x.at[l], ps.at[l], pr.at[l], device_id=(me, lo * 2 + 1 - q), device_id_type=MESH
        )

    def ask(s, who):
        return pltpu.make_async_remote_copy(
            req.at[s], reqin.at[who], rs.at[s], rr.at[who], device_id=(s, col), device_id_type=MESH
        )

    def give(l, d, who, wl):
        return pltpu.make_async_remote_copy(
            o.at[l, d], r.at[wl, who], sends.at[l, d], recvs.at[wl, who],
            device_id=(d, l * 2 + q), device_id_type=MESH,
        )

    swap(0).start()
    swap(1).start()

    @pl.loop(1, N_ROW)
    def _(p):
        ask(lax.rem(me + p, N_ROW), me).start()

    reqin[me] = req[me]

    @pl.loop(1, N_ROW)
    def _(p):
        s = lax.rem(me + p, N_ROW)
        ask(s, s).wait_recv()

    lane = lax.broadcasted_iota(I32, (CAP, 128), 1)
    line = lax.broadcasted_iota(I32, (CAP, 128), 0)

    @pl.loop(0, N_ROW)
    def _(d):
        row = jnp.broadcast_to(reqin[d], (CAP, 128))
        val = jnp.sum(jnp.where(lane == line, row, 0), axis=1, keepdims=True)
        cv[pl.ds(pl.multiple_of(d * CAP, 8), CAP), :] = jnp.broadcast_to(val, (CAP, 128))

    @pl.loop(0, SLOTS // 128)
    def _(b):
        at = pl.ds(pl.multiple_of(b * 128, 128), 128)
        want = cv[at, :]
        for j in range(ROWS // 128):
            here = lax.broadcasted_iota(I32, (128, 128), 1) + j * 128
            perm[at, j * 128 : (j + 1) * 128] = (want == here).astype(F32).astype(BF16)

    for l in range(2):
        swap(l).wait_recv()
        sm[...] = (part[l * 2 + q].astype(F32) + x[l].astype(F32)).astype(BF16)
        of[...] = jnp.dot(perm[...], sm[...], preferred_element_type=F32)

        @pl.loop(0, N_ROW)
        def _(d):
            o[l, d] = of[pl.ds(pl.multiple_of(d * CAP, 8), CAP), :].astype(BF16)

        @pl.loop(1, N_ROW)
        def _(p):
            give(l, lax.rem(me + p, N_ROW), me, lo).start()

    give(1 - lo, me, me, lo).start()
    r[lo, me] = o[lo, me]
    give(lo, me, me, 1 - lo).wait_recv()
    of[pl.ds(pl.multiple_of(me * CAP, 8), CAP), :] = r[0, me].astype(F32) + r[1, me].astype(F32)

    @pl.loop(1, N_ROW)
    def _(p):
        s = lax.rem(me + N_ROW - p, N_ROW)
        for l in range(2):
            give(lo, s, s, l).wait_recv()
        of[pl.ds(pl.multiple_of(s * CAP, 8), CAP), :] = r[0, s].astype(F32) + r[1, s].astype(F32)

    rb[...] = of[...].astype(BF16)
    for p in range(2):
        pick = slotcol[p * 256 : (p + 1) * 256, :]
        sel = jnp.concatenate(
            [
                (pick == lax.broadcasted_iota(I32, (256, 128), 1) + j * 128).astype(F32).astype(BF16)
                for j in range(SLOTS // 128)
            ],
            axis=1,
        )
        schur = jnp.dot(sel, rb[...], preferred_element_type=F32)
        out[p] = (bem[p].astype(F32) - schur).astype(BF16)

    for l in range(2):
        swap(l).wait_send()
    give(1 - lo, me, me, lo).wait_send()

    @pl.loop(1, N_ROW)
    def _(p):
        d = lax.rem(me + p, N_ROW)
        ask(d, me).wait_send()
        for l in range(2):
            give(l, d, me, lo).wait_send()


def route(req, slotcol, part, bem):
    vm = pl.BlockSpec(memory_space=pltpu.VMEM)
    dma = pltpu.SemaphoreType.DMA
    return pl.pallas_call(
        route_kernel,
        out_shape=jax.ShapeDtypeStruct((2, 256, 512), BF16),
        in_specs=[vm] * 4,
        out_specs=vm,
        scratch_shapes=[
            pltpu.VMEM((2, ROWS, 512), BF16),
            pltpu.VMEM((2, N_ROW, CAP, 512), BF16),
            pltpu.VMEM((SLOTS, 512), F32),
            pltpu.VMEM((2, N_ROW, CAP, 512), BF16),
            pltpu.VMEM((N_ROW, 1, 128), I32),
            pltpu.VMEM((SLOTS, 128), I32),
            pltpu.VMEM((SLOTS, ROWS), BF16),
            pltpu.VMEM((ROWS, 512), BF16),
            pltpu.VMEM((SLOTS, 512), BF16),
            dma((2,)), dma((2,)), dma((N_ROW,)), dma((N_ROW,)), dma((2, N_ROW)), dma((2, N_ROW)),
        ],
        compiler_params=pltpu.CompilerParams(collective_id=0, has_side_effects=True, vmem_limit_bytes=56 << 20),
        cost_estimate=pl.CostEstimate(flops=8 << 30, bytes_accessed=60 << 20, transcendentals=0),
        name="route",
    )(req, slotcol, part, bem)


def pack_kernel(a_piv, a_low, *rest):
    outs, (buf, isem, osem) = rest[:6], rest[6:]
    me, col = lax.axis_index("row"), lax.axis_index("col")
    y, x, q = me // 8, (me // 2) % 4, col % 2
    ins = []
    for n in range(6):
        src, j = (a_piv, a_low)[n // 3], n % 3 + 1
        for i in range(4):
            at = (1 - q) * (i * 4 + (x + j) % 4) + q * ((y + j) % 4 * 4 + i)
            ins.append(
                pltpu.make_async_copy(
                    src.at[:, pl.ds(pl.multiple_of(at * 512, 512), 512)], buf.at[n, i], isem.at[n, i]
                )
            )
            ins[-1].start()
    for n in range(6):
        for i in range(4):
            ins[n * 4 + i].wait()
        pltpu.make_async_copy(buf.at[n], outs[n], osem.at[n]).start()
    for n in range(6):
        pltpu.make_async_copy(buf.at[n], outs[n], osem.at[n]).wait()


def pack(a_piv, a_low):
    hbm = pl.BlockSpec(memory_space=pl.ANY)
    return pl.pallas_call(
        pack_kernel,
        out_shape=[jax.ShapeDtypeStruct((4, 256, 512), BF16)] * 6,
        in_specs=[hbm] * 2,
        out_specs=[hbm] * 6,
        scratch_shapes=[
            pltpu.VMEM((6, 4, 256, 512), BF16),
            pltpu.SemaphoreType.DMA((6, 4)),
            pltpu.SemaphoreType.DMA((6,)),
        ],
        compiler_params=pltpu.CompilerParams(vmem_limit_bytes=56 << 20),
        cost_estimate=pl.CostEstimate(flops=0, bytes_accessed=12 << 20, transcendentals=0),
        name="pack",
    )(a_piv, a_low)


def shift(v, j):
    pairs = []
    for r in range(N_ROW):
        y, x, z = r // 8, r // 2 % 4, r % 2
        for c in range(4):
            to = (y * 4 + (x + j) % 4) * 2 + z if c % 2 == 0 else ((y + j) % 4 * 4 + x) * 2 + z
            pairs.append((r * 4 + c, to * 4 + c))
    return lax.ppermute(v, ("row", "col"), pairs)


def panel_kernel(
    asm, a_piv, a_low, p1, p2, p3, l1, l2, l3, out, tiles, b, acc, give, got,
    asem, zs, zr, gs, gr, fs, fr, ss, sr,
):
    me, col = lax.axis_index("row"), lax.axis_index("col")
    y, x, z, q = me // 8, (me // 2) % 4, me % 2, col % 2
    along = (1 - q) * y + q * x

    def on_gather(d):
        return (((y + (1 - q) * d) % 4) * 4 + (x + q * d) % 4) * 2 + z

    def on_scatter(d):
        return (((y + q * d) % 4) * 4 + (x + (1 - q) * d) % 4) * 2 + z

    other = me + 1 - 2 * z
    loads = []
    for n, (own, rest) in enumerate(((a_piv, (p1, p2, p3)), (a_low, (l1, l2, l3)))):
        mine = []
        for i in range(4):
            at = (1 - q) * (i * 4 + x) + q * (y * 4 + i)
            mine.append(
                pltpu.make_async_copy(
                    own.at[:, pl.ds(pl.multiple_of(at * 512, 512), 512)], tiles.at[n, 0, i], asem.at[n, i]
                )
            )
        for j in range(3):
            mine.append(pltpu.make_async_copy(rest[j], tiles.at[n, j + 1], asem.at[n, 4 + j]))
        for load in mine:
            load.start()
        loads.append(mine)

    barrier = pltpu.get_barrier_semaphore()
    peers = [other] + [on_gather(d) for d in (1, 3, 2)] + [on_scatter(d) for d in (1, 3, 2)]
    for peer in peers:
        pl.semaphore_signal(barrier, inc=1, device_id=(peer, col), device_id_type=MESH)

    def send(src, dst, s, r, to):
        copy = pltpu.make_async_remote_copy(
            src, dst, s, r, device_id=(to, col), device_id_type=MESH
        )
        copy.start()
        return copy

    def spot(d, dz):
        return (along + d) % 4 * 2 + (z + dz) % 2

    def phase(n):
        own, pair = spot(0, 0), spot(0, 1)
        sent = []

        def hold(ref, s, r):
            pltpu.make_async_remote_copy(ref, ref, s, r, device_id=(other, col), device_id_type=MESH).wait_recv()

        def piece(j, d, dz):
            lhs = tiles[n, j, (along + d) % 4, :, pl.ds(pl.multiple_of((z + dz) % 2 * 256, 256), 256)]
            return jnp.dot(lhs, b[n, spot(d, dz)].reshape(256, 512), preferred_element_type=F32)

        def add(d, dz):
            @pl.loop(0, 4)
            def _(j):
                acc[j] += piece(j, d, dz)

        for h in range(2):
            sent.append(send(b.at[n, own, h], b.at[n, own, h], zs.at[n, h], zr.at[n, h], other))
        for d in (1, 3, 2):
            sent.append(send(b.at[n, own], b.at[n, own], gs.at[n, d], gr.at[n, d], on_gather(d)))
        for load in loads[n]:
            load.wait()

        @pl.loop(0, 4)
        def _(j):
            acc[j] = piece(j, 0, 0)

        def relay(h):
            hold(b.at[n, pair, h], zs.at[n, h], zr.at[n, h])
            for d in (1, 3, 2):
                sent.append(
                    send(b.at[n, pair, h], b.at[n, pair, h], fs.at[n, d, h], fr.at[n, d, h], on_gather(d))
                )

        def near(d):
            hold(b.at[n, spot(d, 0)], gs.at[n, 4 - d], gr.at[n, 4 - d])
            add(d, 0)

        def far(d):
            for h in range(2):
                hold(b.at[n, spot(d, 1), h], fs.at[n, 4 - d, h], fr.at[n, 4 - d, h])

        relay(0)
        near(3)
        relay(1)
        near(1)
        add(0, 1)
        near(2)
        far(3)
        add(3, 1)
        far(1)
        add(1, 1)
        far(2)
        for j in (2, 1, 3):
            give[n, j] = (acc[j] + piece(j, 2, 1)).astype(BF16)
            sent.append(send(give.at[n, j], got.at[n, j], ss.at[n, j], sr.at[n, j], on_scatter(4 - j)))
        total = acc[0] + piece(0, 2, 1)
        for j in (1, 3, 2):
            hold(got.at[n, j], ss.at[n, j], sr.at[n, j])
        total = total + (got[n, 1].astype(F32) + got[n, 3].astype(F32) + got[n, 2].astype(F32))
        return total, sent

    b[0, spot(0, 0)] = asm[0].reshape(2, 128, 512)
    pl.semaphore_wait(barrier, 7)
    total, sent = phase(0)
    solved = total.astype(BF16)
    b[1, spot(0, 0)] = solved.reshape(2, 128, 512)
    out[0] = solved
    total, more = phase(1)
    out[1] = (asm[1].astype(F32) - total).astype(BF16)
    for copy in sent + more:
        copy.wait_send()


def panel(asm, a_piv, a_low, moved):
    vm = pl.BlockSpec(memory_space=pltpu.VMEM)
    hbm = pl.BlockSpec(memory_space=pl.ANY)
    dma = pltpu.SemaphoreType.DMA
    return pl.pallas_call(
        panel_kernel,
        out_shape=jax.ShapeDtypeStruct((2, 256, 512), BF16),
        in_specs=[vm] + [hbm] * 8,
        out_specs=vm,
        scratch_shapes=[
            pltpu.VMEM((2, 4, 4, 256, 512), BF16),
            pltpu.VMEM((2, 8, 2, 128, 512), BF16),
            pltpu.VMEM((4, 256, 512), F32),
            pltpu.VMEM((2, 4, 256, 512), BF16),
            pltpu.VMEM((2, 4, 256, 512), BF16),
            dma((2, 7)), dma((2, 2)), dma((2, 2)), dma((2, 4)), dma((2, 4)), dma((2, 4, 2)), dma((2, 4, 2)),
            dma((2, 4)), dma((2, 4)),
        ],
        compiler_params=pltpu.CompilerParams(collective_id=1, has_side_effects=True, vmem_limit_bytes=56 << 20),
        cost_estimate=pl.CostEstimate(flops=4 << 30, bytes_accessed=64 << 20, transcendentals=0),
        name="panel",
    )(asm, a_piv, a_low, *moved)


def routes(surface_map):
    flat = surface_map.reshape(-1)
    owner, local = flat // ROWS, flat % ROWS
    n = flat.shape[0]
    ids = jnp.arange(n, dtype=I32)
    before = (owner[:, None] == owner[None, :]) & (ids[None, :] < ids[:, None])
    slot = owner * CAP + jnp.sum(before.astype(I32), axis=1)
    want = jnp.arange(N_ROW * 128, dtype=I32)
    at = jnp.where(want % 128 < CAP, (want // 128) * CAP + want % 128, -1)
    hit = at[:, None] == slot[None, :]
    req = jnp.sum(jnp.where(hit, local[None, :] + 1, 0), axis=1) - 1
    return req.reshape(N_ROW, 1, 128), jnp.broadcast_to(slot[:, None], (n, 128))


def per_device(front_inverse, tiles, tile_row, tile_col, surface_map, bem, pivot, below):
    moved = [shift(v, n % 3 + 1) for n, v in enumerate(pack(pivot, below))]
    req, slotcol = routes(surface_map)
    part = front(tile_row, tile_col, front_inverse, tiles)
    asm = route(req, slotcol, part, bem)
    return panel(asm, pivot, below, moved)


def solution(mesh):
    placed = (
        P("row", "col"),
        P("col", None, None),
        P("col"),
        P("col"),
        P(None, "row"),
        P(None, "row", "col"),
        P("row", None),
        P("row", None),
    )
    return jax.shard_map(
        per_device, mesh=mesh, in_specs=placed, out_specs=P(None, "row", "col"), check_vma=False
    )
```

```python
import jax
import jax.numpy as jnp
from jax import lax
from jax.experimental import pallas as pl
from jax.experimental.pallas import tpu as pltpu
from jax.sharding import PartitionSpec as P

MESH = pl.DeviceIdType.MESH
F32, BF16, I32 = jnp.float32, jnp.bfloat16, jnp.int32
N_ROW, CAP = 32, 24
SLOTS = N_ROW * CAP
ROWS = 768
GROUP = 4
TILES = 192
PAIRS = 8
UNROLL = 3
CHUNKS = (TILES + PAIRS * (GROUP - 1)) // GROUP + UNROLL
VMEM = 63 << 20


def front_kernel(trow, tcol, f_hbm, t_hbm, out_hbm, f, w, acc, ob, cell, left, right, lrs, ccol, fsem, tsem, osem):
    loads = [
        pltpu.make_async_copy(t_hbm, w.at[pl.ds(0, TILES)], tsem),
        pltpu.make_async_copy(f_hbm, f, fsem),
    ]
    for load in loads:
        load.start()
    first = lax.axis_index("col") * 48

    @pl.loop(0, PAIRS * 12)
    def _(i):
        for u in range(8):
            cell[i * 8 + u] = TILES

    @pl.loop(0, TILES)
    def _(i):
        b = tcol[i]
        cell[(b // 2) * 96 + (trow[i] - first) * 2 + b % 2] = i

    def finish(n):
        for g in range(GROUP):
            left[n + g] = TILES
            right[n + g] = TILES
            lrs[n + g] = 0
        return (n + GROUP - 1) // GROUP * GROUP

    def place(b, n):
        def visit(lr, n):
            one, two = cell[b * 96 + lr * 2], cell[b * 96 + lr * 2 + 1]
            left[n], right[n], lrs[n] = one, two, lr
            return n + jnp.where(one + two == 2 * TILES, 0, 1)

        end = finish(lax.fori_loop(0, 48, visit, n, unroll=4))

        def name(c, _):
            ccol[c] = b
            return 0

        lax.fori_loop(n // GROUP, end // GROUP, name, 0)
        return end

    total = lax.fori_loop(0, PAIRS, place, 0) // GROUP
    for u in range(UNROLL - 1):
        finish((total + u) * GROUP)
        ccol[total + u] = 0
    w[TILES] = jnp.zeros((128, 128), BF16)
    acc[...] = jnp.zeros_like(acc)
    for load in loads:
        load.wait()

    @pl.loop(0, (total + UNROLL - 1) // UNROLL)
    def _(it):
        for u in range(UNROLL):
            c = it * UNROLL + u
            lhs, rhs = [], []
            for g in range(GROUP):
                k = c * GROUP + g
                lhs.append(f[:, pl.ds(pl.multiple_of(lrs[k] * 128, 128), 128)])
                rhs.append(jnp.concatenate([w[left[k]], w[right[k]]], axis=1))
            at = pl.multiple_of(ccol[c] * 256, 256)
            acc[:, pl.ds(at, 256)] += jnp.dot(
                jnp.concatenate(lhs, axis=1), jnp.concatenate(rhs, axis=0), preferred_element_type=F32
            )

    for k in range(4):
        ob[k] = acc[:, k * 512 : (k + 1) * 512].astype(BF16)
        pltpu.make_async_copy(ob.at[k], out_hbm.at[k], osem.at[k]).start()
    for k in range(4):
        pltpu.make_async_copy(ob.at[k], out_hbm.at[k], osem.at[k]).wait()


def front(trow, tcol, f, tiles):
    smem = pl.BlockSpec(memory_space=pltpu.SMEM)
    hbm = pl.BlockSpec(memory_space=pl.ANY)
    listed = pltpu.SMEM((CHUNKS * GROUP,), I32)
    return pl.pallas_call(
        front_kernel,
        out_shape=jax.ShapeDtypeStruct((4, ROWS, 512), BF16),
        in_specs=[smem, smem, hbm, hbm],
        out_specs=hbm,
        scratch_shapes=[
            pltpu.VMEM((ROWS, 6144), BF16),
            pltpu.VMEM((TILES + 1, 128, 128), BF16),
            pltpu.VMEM((ROWS, 2048), F32),
            pltpu.VMEM((4, ROWS, 512), BF16),
            pltpu.SMEM((PAIRS * 96,), I32),
            listed, listed, listed,
            pltpu.SMEM((CHUNKS,), I32),
            pltpu.SemaphoreType.DMA,
            pltpu.SemaphoreType.DMA,
            pltpu.SemaphoreType.DMA((4,)),
        ],
        compiler_params=pltpu.CompilerParams(vmem_limit_bytes=VMEM),
        cost_estimate=pl.CostEstimate(flops=20 << 30, bytes_accessed=60 << 20, transcendentals=0),
        name="front",
    )(trow, tcol, f, tiles)


def route_kernel(
    smap, part, bem, out, own, x, o, of, r, req, reqin, table, high, low, slotcol, cv, perm, sm, rb,
    os, ps, pr, rs, rr, sends, recvs,
):
    me, col = lax.axis_index("row"), lax.axis_index("col")
    q, lo = col % 2, col // 2
    barrier = pltpu.get_barrier_semaphore()

    def tell(a, b):
        pl.semaphore_signal(barrier, inc=1, device_id=(a, b), device_id_type=MESH)

    tell(me, lo * 2 + 1 - q)
    tell(me, (1 - lo) * 2 + q)

    @pl.loop(1, N_ROW)
    def _(p):
        for l in range(2):
            tell(lax.rem(me + p, N_ROW), l * 2 + q)

    mine = [pltpu.make_async_copy(part.at[l * 2 + q], own.at[l], os.at[l]) for l in range(2)]
    for copy in mine:
        copy.start()
    want = jnp.concatenate([smap[0:1, :], smap[1:2, :]], axis=1)
    owner = jnp.zeros_like(want)
    for k in range(1, N_ROW):
        owner += (want >= k * ROWS).astype(I32)
    local = want - owner * ROWS
    wide = want.shape[1]

    @pl.loop(0, wide // 64)
    def _(b):
        at = pl.ds(pl.multiple_of(b * 64, 64), 64)
        here = lax.broadcasted_iota(I32, (64, wide), 0) + b * 64
        lane = lax.broadcasted_iota(I32, (64, wide), 1)
        all_owner = jnp.broadcast_to(owner, (64, wide))
        own_col = jnp.sum(jnp.where(here == lane, all_owner, 0), axis=1, keepdims=True)
        value = jnp.sum(jnp.where(here == lane, jnp.broadcast_to(local, (64, wide)), 0), axis=1, keepdims=True) + 1
        before = jnp.where((own_col == all_owner) & (lane < here), 1, 0)
        rank = jnp.sum(before, axis=1, keepdims=True)
        slotcol[at, :] = jnp.broadcast_to(own_col * CAP + rank, (64, 128))
        hit = rank == lax.broadcasted_iota(I32, (64, 128), 1)
        high[at, :] = jnp.where(hit, value >> 5, 0).astype(F32).astype(BF16)
        low[at, :] = jnp.where(hit, value & 31, 0).astype(F32).astype(BF16)

    of_source = (jnp.broadcast_to(owner, (N_ROW, wide)) == lax.broadcasted_iota(I32, (N_ROW, wide), 0))
    of_source = of_source.astype(F32).astype(BF16)
    table[...] = (
        32.0 * jnp.dot(of_source, high[...], preferred_element_type=F32)
        + jnp.dot(of_source, low[...], preferred_element_type=F32)
    ).astype(I32) - 1

    @pl.loop(0, N_ROW)
    def _(s):
        req[s] = table[pl.ds(s, 1), :]

    pl.semaphore_wait(barrier, 64)

    def swap(l):
        return pltpu.make_async_remote_copy(
            part.at[l * 2 + 1 - q], x.at[l], ps.at[l], pr.at[l], device_id=(me, lo * 2 + 1 - q), device_id_type=MESH
        )

    def ask(s, who):
        return pltpu.make_async_remote_copy(
            req.at[s], reqin.at[who], rs.at[s], rr.at[who], device_id=(s, col), device_id_type=MESH
        )

    def give(l, d, who, wl):
        return pltpu.make_async_remote_copy(
            o.at[l, d], r.at[wl, who], sends.at[l, d], recvs.at[wl, who],
            device_id=(d, l * 2 + q), device_id_type=MESH,
        )

    swap(0).start()
    swap(1).start()

    @pl.loop(1, N_ROW)
    def _(p):
        ask(lax.rem(me + p, N_ROW), me).start()

    reqin[me] = req[me]

    @pl.loop(1, N_ROW)
    def _(p):
        s = lax.rem(me + p, N_ROW)
        ask(s, s).wait_recv()

    lane = lax.broadcasted_iota(I32, (CAP, 128), 1)
    line = lax.broadcasted_iota(I32, (CAP, 128), 0)

    @pl.loop(0, N_ROW)
    def _(d):
        row = jnp.broadcast_to(reqin[d], (CAP, 128))
        val = jnp.sum(jnp.where(lane == line, row, 0), axis=1, keepdims=True)
        cv[pl.ds(pl.multiple_of(d * CAP, 8), CAP), :] = jnp.broadcast_to(val, (CAP, 128))

    @pl.loop(0, SLOTS // 128)
    def _(b):
        at = pl.ds(pl.multiple_of(b * 128, 128), 128)
        want = cv[at, :]
        for j in range(ROWS // 128):
            here = lax.broadcasted_iota(I32, (128, 128), 1) + j * 128
            perm[at, j * 128 : (j + 1) * 128] = (want == here).astype(F32).astype(BF16)

    for l in range(2):
        mine[l].wait()
        swap(l).wait_recv()
        sm[...] = (own[l].astype(F32) + x[l].astype(F32)).astype(BF16)
        of[...] = jnp.dot(perm[...], sm[...], preferred_element_type=F32)

        @pl.loop(0, N_ROW)
        def _(d):
            o[l, d] = of[pl.ds(pl.multiple_of(d * CAP, 8), CAP), :].astype(BF16)

        @pl.loop(1, N_ROW)
        def _(p):
            give(l, lax.rem(me + p, N_ROW), me, lo).start()

    give(1 - lo, me, me, lo).start()
    r[lo, me] = o[lo, me]
    give(lo, me, me, 1 - lo).wait_recv()
    of[pl.ds(pl.multiple_of(me * CAP, 8), CAP), :] = r[0, me].astype(F32) + r[1, me].astype(F32)

    @pl.loop(1, N_ROW)
    def _(p):
        s = lax.rem(me + N_ROW - p, N_ROW)
        for l in range(2):
            give(lo, s, s, l).wait_recv()
        of[pl.ds(pl.multiple_of(s * CAP, 8), CAP), :] = r[0, s].astype(F32) + r[1, s].astype(F32)

    rb[...] = of[...].astype(BF16)
    for p in range(2):
        pick = slotcol[p * 256 : (p + 1) * 256, :]
        sel = jnp.concatenate(
            [
                (pick == lax.broadcasted_iota(I32, (256, 128), 1) + j * 128).astype(F32).astype(BF16)
                for j in range(SLOTS // 128)
            ],
            axis=1,
        )
        schur = jnp.dot(sel, rb[...], preferred_element_type=F32)
        out[p] = (bem[p].astype(F32) - schur).astype(BF16)

    for l in range(2):
        swap(l).wait_send()
    give(1 - lo, me, me, lo).wait_send()

    @pl.loop(1, N_ROW)
    def _(p):
        d = lax.rem(me + p, N_ROW)
        ask(d, me).wait_send()
        for l in range(2):
            give(l, d, me, lo).wait_send()


def route(smap, part, bem):
    hbm = pl.BlockSpec(memory_space=pl.ANY)
    vm = pl.BlockSpec(memory_space=pltpu.VMEM)
    dma = pltpu.SemaphoreType.DMA
    return pl.pallas_call(
        route_kernel,
        out_shape=jax.ShapeDtypeStruct((2, 256, 512), BF16),
        in_specs=[vm, hbm, vm],
        out_specs=vm,
        scratch_shapes=[
            pltpu.VMEM((2, ROWS, 512), BF16),
            pltpu.VMEM((2, ROWS, 512), BF16),
            pltpu.VMEM((2, N_ROW, CAP, 512), BF16),
            pltpu.VMEM((SLOTS, 512), F32),
            pltpu.VMEM((2, N_ROW, CAP, 512), BF16),
            pltpu.VMEM((N_ROW, 1, 128), I32),
            pltpu.VMEM((N_ROW, 1, 128), I32),
            pltpu.VMEM((N_ROW, 128), I32),
            pltpu.VMEM((512, 128), BF16),
            pltpu.VMEM((512, 128), BF16),
            pltpu.VMEM((512, 128), I32),
            pltpu.VMEM((SLOTS, 128), I32),
            pltpu.VMEM((SLOTS, ROWS), BF16),
            pltpu.VMEM((ROWS, 512), BF16),
            pltpu.VMEM((SLOTS, 512), BF16),
            dma((2,)), dma((2,)), dma((2,)), dma((N_ROW,)), dma((N_ROW,)), dma((2, N_ROW)), dma((2, N_ROW)),
        ],
        compiler_params=pltpu.CompilerParams(collective_id=0, has_side_effects=True, vmem_limit_bytes=VMEM),
        cost_estimate=pl.CostEstimate(flops=8 << 30, bytes_accessed=60 << 20, transcendentals=0),
        name="route",
    )(smap, part, bem)


def pack_kernel(a_piv, a_low, *rest):
    outs, (buf, isem, osem) = rest[:3], rest[3:]
    me, col = lax.axis_index("row"), lax.axis_index("col")
    y, x, q = me // 8, (me // 2) % 4, col % 2
    ins = []
    for n in range(6):
        src, j = (a_piv, a_low)[n % 2], n // 2 + 1
        for i in range(4):
            at = (1 - q) * (i * 4 + (x + j) % 4) + q * ((y + j) % 4 * 4 + i)
            ins.append(
                pltpu.make_async_copy(
                    src.at[:, pl.ds(pl.multiple_of(at * 512, 512), 512)], buf.at[n, i], isem.at[n, i]
                )
            )
            ins[-1].start()
    for n in range(6):
        for i in range(4):
            ins[n * 4 + i].wait()
        pltpu.make_async_copy(buf.at[n], outs[n // 2].at[n % 2], osem.at[n]).start()
    for n in range(6):
        pltpu.make_async_copy(buf.at[n], outs[n // 2].at[n % 2], osem.at[n]).wait()


def pack(a_piv, a_low):
    hbm = pl.BlockSpec(memory_space=pl.ANY)
    return pl.pallas_call(
        pack_kernel,
        out_shape=[jax.ShapeDtypeStruct((2, 4, 256, 512), BF16)] * 3,
        in_specs=[hbm] * 2,
        out_specs=[hbm] * 3,
        scratch_shapes=[
            pltpu.VMEM((6, 4, 256, 512), BF16),
            pltpu.SemaphoreType.DMA((6, 4)),
            pltpu.SemaphoreType.DMA((6,)),
        ],
        compiler_params=pltpu.CompilerParams(vmem_limit_bytes=VMEM),
        cost_estimate=pl.CostEstimate(flops=0, bytes_accessed=12 << 20, transcendentals=0),
        name="pack",
    )(a_piv, a_low)


def shift(v, j):
    pairs = []
    for r in range(N_ROW):
        y, x, z = r // 8, r // 2 % 4, r % 2
        for c in range(4):
            to = (y * 4 + (x + j) % 4) * 2 + z if c % 2 == 0 else ((y + j) % 4 * 4 + x) * 2 + z
            pairs.append((r * 4 + c, to * 4 + c))
    return lax.ppermute(v, ("row", "col"), pairs)


def panel_kernel(
    asm, a_piv, a_low, m1, m2, m3, out, tiles, b, acc, give, got,
    asem, zs, zr, gs, gr, fs, fr, ss, sr,
):
    me, col = lax.axis_index("row"), lax.axis_index("col")
    y, x, z, q = me // 8, (me // 2) % 4, me % 2, col % 2
    along = (1 - q) * y + q * x

    def on_gather(d):
        return (((y + (1 - q) * d) % 4) * 4 + (x + q * d) % 4) * 2 + z

    def on_scatter(d):
        return (((y + q * d) % 4) * 4 + (x + (1 - q) * d) % 4) * 2 + z

    other = me + 1 - 2 * z
    loads = []
    for n, own in enumerate((a_piv, a_low)):
        mine = []
        for i in range(4):
            at = (1 - q) * (i * 4 + x) + q * (y * 4 + i)
            mine.append(
                pltpu.make_async_copy(
                    own.at[:, pl.ds(pl.multiple_of(at * 512, 512), 512)], tiles.at[n, 0, i], asem.at[n, i]
                )
            )
        for j in range(3):
            mine.append(pltpu.make_async_copy((m1, m2, m3)[j].at[n], tiles.at[n, j + 1], asem.at[n, 4 + j]))
        for load in mine:
            load.start()
        loads.append(mine)

    barrier = pltpu.get_barrier_semaphore()
    peers = [other] + [on_gather(d) for d in (1, 3, 2)] + [on_scatter(d) for d in (1, 3, 2)]
    for peer in peers:
        pl.semaphore_signal(barrier, inc=1, device_id=(peer, col), device_id_type=MESH)

    def send(src, dst, s, r, to):
        copy = pltpu.make_async_remote_copy(
            src, dst, s, r, device_id=(to, col), device_id_type=MESH
        )
        copy.start()
        return copy

    def spot(d, dz):
        return (along + d) % 4 * 2 + (z + dz) % 2

    def phase(n):
        own, pair = spot(0, 0), spot(0, 1)
        sent = []

        def hold(ref, s, r):
            pltpu.make_async_remote_copy(ref, ref, s, r, device_id=(other, col), device_id_type=MESH).wait_recv()

        def piece(j, d, dz):
            lhs = tiles[n, j, (along + d) % 4, :, pl.ds(pl.multiple_of((z + dz) % 2 * 256, 256), 256)]
            return jnp.dot(lhs, b[n, spot(d, dz)].reshape(256, 512), preferred_element_type=F32)

        def add(d, dz):
            @pl.loop(0, 4)
            def _(j):
                acc[j] += piece(j, d, dz)

        for h in range(2):
            sent.append(send(b.at[n, own, h], b.at[n, own, h], zs.at[n, h], zr.at[n, h], other))
        for d in (1, 3, 2):
            sent.append(send(b.at[n, own], b.at[n, own], gs.at[n, d], gr.at[n, d], on_gather(d)))
        for load in loads[n]:
            load.wait()

        @pl.loop(0, 4)
        def _(j):
            acc[j] = piece(j, 0, 0)

        def relay(h):
            hold(b.at[n, pair, h], zs.at[n, h], zr.at[n, h])
            for d in (1, 3, 2):
                sent.append(
                    send(b.at[n, pair, h], b.at[n, pair, h], fs.at[n, d, h], fr.at[n, d, h], on_gather(d))
                )

        def near(d):
            hold(b.at[n, spot(d, 0)], gs.at[n, 4 - d], gr.at[n, 4 - d])
            add(d, 0)

        def far(d):
            for h in range(2):
                hold(b.at[n, spot(d, 1), h], fs.at[n, 4 - d, h], fr.at[n, 4 - d, h])

        relay(0)
        near(3)
        relay(1)
        near(1)
        add(0, 1)
        near(2)
        far(3)
        add(3, 1)
        far(1)
        add(1, 1)
        far(2)
        for j in (2, 1, 3):
            give[n, j] = (acc[j] + piece(j, 2, 1)).astype(BF16)
            sent.append(send(give.at[n, j], got.at[n, j], ss.at[n, j], sr.at[n, j], on_scatter(4 - j)))
        total = acc[0] + piece(0, 2, 1)
        for j in (1, 3, 2):
            hold(got.at[n, j], ss.at[n, j], sr.at[n, j])
        total = total + (got[n, 1].astype(F32) + got[n, 3].astype(F32) + got[n, 2].astype(F32))
        return total, sent

    b[0, spot(0, 0)] = asm[0].reshape(2, 128, 512)
    pl.semaphore_wait(barrier, 7)
    total, sent = phase(0)
    solved = total.astype(BF16)
    b[1, spot(0, 0)] = solved.reshape(2, 128, 512)
    out[0] = solved
    total, more = phase(1)
    out[1] = (asm[1].astype(F32) - total).astype(BF16)
    for copy in sent + more:
        copy.wait_send()


def panel(asm, a_piv, a_low, moved):
    vm = pl.BlockSpec(memory_space=pltpu.VMEM)
    hbm = pl.BlockSpec(memory_space=pl.ANY)
    dma = pltpu.SemaphoreType.DMA
    return pl.pallas_call(
        panel_kernel,
        out_shape=jax.ShapeDtypeStruct((2, 256, 512), BF16),
        in_specs=[vm] + [hbm] * 5,
        out_specs=vm,
        scratch_shapes=[
            pltpu.VMEM((2, 4, 4, 256, 512), BF16),
            pltpu.VMEM((2, 8, 2, 128, 512), BF16),
            pltpu.VMEM((4, 256, 512), F32),
            pltpu.VMEM((2, 4, 256, 512), BF16),
            pltpu.VMEM((2, 4, 256, 512), BF16),
            dma((2, 7)), dma((2, 2)), dma((2, 2)), dma((2, 4)), dma((2, 4)), dma((2, 4, 2)), dma((2, 4, 2)),
            dma((2, 4)), dma((2, 4)),
        ],
        compiler_params=pltpu.CompilerParams(collective_id=1, has_side_effects=True, vmem_limit_bytes=VMEM),
        cost_estimate=pl.CostEstimate(flops=4 << 30, bytes_accessed=64 << 20, transcendentals=0),
        name="panel",
    )(asm, a_piv, a_low, *moved)


def per_device(front_inverse, tiles, tile_row, tile_col, surface_map, bem, pivot, below):
    moved = [shift(v, n + 1) for n, v in enumerate(pack(pivot, below))]
    part = front(tile_row, tile_col, front_inverse, tiles)
    asm = route(surface_map, part, bem)
    return panel(asm, pivot, below, moved)


def solution(mesh):
    placed = (
        P("row", "col"),
        P("col", None, None),
        P("col"),
        P("col"),
        P(None, "row"),
        P(None, "row", "col"),
        P("row", None),
        P("row", None),
    )
    return jax.shard_map(
        per_device, mesh=mesh, in_specs=placed, out_specs=P(None, "row", "col"), check_vma=False
    )
```

```python
import functools

import jax
import jax.numpy as jnp
from jax import lax
from jax.experimental import pallas as pl
from jax.experimental.pallas import tpu as pltpu
from jax.sharding import PartitionSpec as P

MESH = pl.DeviceIdType.MESH
F32, BF16, I32 = jnp.float32, jnp.bfloat16, jnp.int32
N_ROW, CAP = 32, 24
SLOTS = N_ROW * CAP
ROWS = 768
GROUP = 4
TILES = 192
PAIRS = 8
UNROLL = 3
CHUNKS = (TILES + PAIRS * (GROUP - 1)) // GROUP + UNROLL
VMEM = 63 << 20


def front_kernel(trow, tcol, f_hbm, t_hbm, out_hbm, f, w, acc, ob, cell, left, right, lrs, ccol, fsem, tsem, osem):
    loads = [
        pltpu.make_async_copy(t_hbm, w.at[pl.ds(0, TILES)], tsem),
        pltpu.make_async_copy(f_hbm, f, fsem),
    ]
    for load in loads:
        load.start()
    first = lax.axis_index("col") * 48

    @pl.loop(0, PAIRS * 12)
    def _(i):
        for u in range(8):
            cell[i * 8 + u] = TILES

    @pl.loop(0, TILES)
    def _(i):
        b = tcol[i]
        cell[(b // 2) * 96 + (trow[i] - first) * 2 + b % 2] = i

    def finish(n):
        for g in range(GROUP):
            left[n + g] = TILES
            right[n + g] = TILES
            lrs[n + g] = 0
        return (n + GROUP - 1) // GROUP * GROUP

    def place(b, n):
        def visit(lr, n):
            one, two = cell[b * 96 + lr * 2], cell[b * 96 + lr * 2 + 1]
            left[n], right[n], lrs[n] = one, two, lr
            return n + jnp.where(one + two == 2 * TILES, 0, 1)

        end = finish(lax.fori_loop(0, 48, visit, n, unroll=4))

        def name(c, _):
            ccol[c] = b
            return 0

        lax.fori_loop(n // GROUP, end // GROUP, name, 0)
        return end

    total = lax.fori_loop(0, PAIRS, place, 0) // GROUP
    for u in range(UNROLL - 1):
        finish((total + u) * GROUP)
        ccol[total + u] = 0
    w[TILES] = jnp.zeros((128, 128), BF16)
    acc[...] = jnp.zeros_like(acc)
    for load in loads:
        load.wait()

    @pl.loop(0, (total + UNROLL - 1) // UNROLL)
    def _(it):
        for u in range(UNROLL):
            c = it * UNROLL + u
            lhs, rhs = [], []
            for g in range(GROUP):
                k = c * GROUP + g
                lhs.append(f[:, pl.ds(pl.multiple_of(lrs[k] * 128, 128), 128)])
                rhs.append(jnp.concatenate([w[left[k]], w[right[k]]], axis=1))
            at = pl.multiple_of(ccol[c] * 256, 256)
            acc[:, pl.ds(at, 256)] += jnp.dot(
                jnp.concatenate(lhs, axis=1), jnp.concatenate(rhs, axis=0), preferred_element_type=F32
            )

    for k in range(4):
        ob[k] = acc[:, k * 512 : (k + 1) * 512].astype(BF16)
        pltpu.make_async_copy(ob.at[k], out_hbm.at[k], osem.at[k]).start()
    for k in range(4):
        pltpu.make_async_copy(ob.at[k], out_hbm.at[k], osem.at[k]).wait()


def front(trow, tcol, f, tiles):
    smem = pl.BlockSpec(memory_space=pltpu.SMEM)
    hbm = pl.BlockSpec(memory_space=pl.ANY)
    listed = pltpu.SMEM((CHUNKS * GROUP,), I32)
    return pl.pallas_call(
        front_kernel,
        out_shape=jax.ShapeDtypeStruct((4, ROWS, 512), BF16),
        in_specs=[smem, smem, hbm, hbm],
        out_specs=hbm,
        scratch_shapes=[
            pltpu.VMEM((ROWS, 6144), BF16),
            pltpu.VMEM((TILES + 1, 128, 128), BF16),
            pltpu.VMEM((ROWS, 2048), F32),
            pltpu.VMEM((4, ROWS, 512), BF16),
            pltpu.SMEM((PAIRS * 96,), I32),
            listed, listed, listed,
            pltpu.SMEM((CHUNKS,), I32),
            pltpu.SemaphoreType.DMA,
            pltpu.SemaphoreType.DMA,
            pltpu.SemaphoreType.DMA((4,)),
        ],
        compiler_params=pltpu.CompilerParams(vmem_limit_bytes=VMEM),
        cost_estimate=pl.CostEstimate(flops=20 << 30, bytes_accessed=60 << 20, transcendentals=0),
        name="front",
    )(trow, tcol, f, tiles)


def route_kernel(
    smap, part, bem, out, own, x, o, of, r, req, reqin, table, high, low, slotcol, cv, perm, sm, rb,
    os, ps, pr, rs, rr, sends, recvs,
):
    me, col = lax.axis_index("row"), lax.axis_index("col")
    q, lo = col % 2, col // 2
    barrier = pltpu.get_barrier_semaphore()

    def tell(a, b):
        pl.semaphore_signal(barrier, inc=1, device_id=(a, b), device_id_type=MESH)

    tell(me, lo * 2 + 1 - q)
    tell(me, (1 - lo) * 2 + q)

    @pl.loop(1, N_ROW)
    def _(p):
        for l in range(2):
            tell(lax.rem(me + p, N_ROW), l * 2 + q)

    mine = [pltpu.make_async_copy(part.at[l * 2 + q], own.at[l], os.at[l]) for l in range(2)]
    for copy in mine:
        copy.start()
    want = jnp.concatenate([smap[0:1, :], smap[1:2, :]], axis=1)
    owner = jnp.zeros_like(want)
    for k in range(1, N_ROW):
        owner += (want >= k * ROWS).astype(I32)
    local = want - owner * ROWS
    wide = want.shape[1]

    @pl.loop(0, wide // 64)
    def _(b):
        at = pl.ds(pl.multiple_of(b * 64, 64), 64)
        here = lax.broadcasted_iota(I32, (64, wide), 0) + b * 64
        lane = lax.broadcasted_iota(I32, (64, wide), 1)
        all_owner = jnp.broadcast_to(owner, (64, wide))
        own_col = jnp.sum(jnp.where(here == lane, all_owner, 0), axis=1, keepdims=True)
        value = jnp.sum(jnp.where(here == lane, jnp.broadcast_to(local, (64, wide)), 0), axis=1, keepdims=True) + 1
        before = jnp.where((own_col == all_owner) & (lane < here), 1, 0)
        rank = jnp.sum(before, axis=1, keepdims=True)
        slotcol[at, :] = jnp.broadcast_to(own_col * CAP + rank, (64, 128))
        hit = rank == lax.broadcasted_iota(I32, (64, 128), 1)
        high[at, :] = jnp.where(hit, value >> 5, 0).astype(F32).astype(BF16)
        low[at, :] = jnp.where(hit, value & 31, 0).astype(F32).astype(BF16)

    of_source = (jnp.broadcast_to(owner, (N_ROW, wide)) == lax.broadcasted_iota(I32, (N_ROW, wide), 0))
    of_source = of_source.astype(F32).astype(BF16)
    table[...] = (
        32.0 * jnp.dot(of_source, high[...], preferred_element_type=F32)
        + jnp.dot(of_source, low[...], preferred_element_type=F32)
    ).astype(I32) - 1

    @pl.loop(0, N_ROW)
    def _(s):
        req[s] = table[pl.ds(s, 1), :]

    pl.semaphore_wait(barrier, 64)

    def swap(l):
        return pltpu.make_async_remote_copy(
            part.at[l * 2 + 1 - q], x.at[l], ps.at[l], pr.at[l], device_id=(me, lo * 2 + 1 - q), device_id_type=MESH
        )

    def ask(s, who):
        return pltpu.make_async_remote_copy(
            req.at[s], reqin.at[who], rs.at[s], rr.at[who], device_id=(s, col), device_id_type=MESH
        )

    def give(l, d, who, wl):
        return pltpu.make_async_remote_copy(
            o.at[l, d], r.at[wl, who], sends.at[l, d], recvs.at[wl, who],
            device_id=(d, l * 2 + q), device_id_type=MESH,
        )

    swap(0).start()
    swap(1).start()

    @pl.loop(1, N_ROW)
    def _(p):
        ask(lax.rem(me + p, N_ROW), me).start()

    reqin[me] = req[me]

    @pl.loop(1, N_ROW)
    def _(p):
        s = lax.rem(me + p, N_ROW)
        ask(s, s).wait_recv()

    lane = lax.broadcasted_iota(I32, (CAP, 128), 1)
    line = lax.broadcasted_iota(I32, (CAP, 128), 0)

    @pl.loop(0, N_ROW)
    def _(d):
        row = jnp.broadcast_to(reqin[d], (CAP, 128))
        val = jnp.sum(jnp.where(lane == line, row, 0), axis=1, keepdims=True)
        cv[pl.ds(pl.multiple_of(d * CAP, 8), CAP), :] = jnp.broadcast_to(val, (CAP, 128))

    @pl.loop(0, SLOTS // 128)
    def _(b):
        at = pl.ds(pl.multiple_of(b * 128, 128), 128)
        want = cv[at, :]
        for j in range(ROWS // 128):
            here = lax.broadcasted_iota(I32, (128, 128), 1) + j * 128
            perm[at, j * 128 : (j + 1) * 128] = (want == here).astype(F32).astype(BF16)

    for l in range(2):
        mine[l].wait()
        swap(l).wait_recv()
        sm[...] = (own[l].astype(F32) + x[l].astype(F32)).astype(BF16)
        of[...] = jnp.dot(perm[...], sm[...], preferred_element_type=F32)

        @pl.loop(0, N_ROW)
        def _(d):
            o[l, d] = of[pl.ds(pl.multiple_of(d * CAP, 8), CAP), :].astype(BF16)

        @pl.loop(1, N_ROW)
        def _(p):
            give(l, lax.rem(me + p, N_ROW), me, lo).start()

    give(1 - lo, me, me, lo).start()
    r[lo, me] = o[lo, me]
    give(lo, me, me, 1 - lo).wait_recv()
    of[pl.ds(pl.multiple_of(me * CAP, 8), CAP), :] = r[0, me].astype(F32) + r[1, me].astype(F32)

    @pl.loop(1, N_ROW)
    def _(p):
        s = lax.rem(me + N_ROW - p, N_ROW)
        for l in range(2):
            give(lo, s, s, l).wait_recv()
        of[pl.ds(pl.multiple_of(s * CAP, 8), CAP), :] = r[0, s].astype(F32) + r[1, s].astype(F32)

    rb[...] = of[...].astype(BF16)
    for p in range(2):
        pick = slotcol[p * 256 : (p + 1) * 256, :]
        sel = jnp.concatenate(
            [
                (pick == lax.broadcasted_iota(I32, (256, 128), 1) + j * 128).astype(F32).astype(BF16)
                for j in range(SLOTS // 128)
            ],
            axis=1,
        )
        schur = jnp.dot(sel, rb[...], preferred_element_type=F32)
        out[p] = (bem[p].astype(F32) - schur).astype(BF16)

    for l in range(2):
        swap(l).wait_send()
    give(1 - lo, me, me, lo).wait_send()

    @pl.loop(1, N_ROW)
    def _(p):
        d = lax.rem(me + p, N_ROW)
        ask(d, me).wait_send()
        for l in range(2):
            give(l, d, me, lo).wait_send()


def route(smap, part, bem):
    hbm = pl.BlockSpec(memory_space=pl.ANY)
    vm = pl.BlockSpec(memory_space=pltpu.VMEM)
    dma = pltpu.SemaphoreType.DMA
    return pl.pallas_call(
        route_kernel,
        out_shape=jax.ShapeDtypeStruct((2, 256, 512), BF16),
        in_specs=[vm, hbm, vm],
        out_specs=vm,
        scratch_shapes=[
            pltpu.VMEM((2, ROWS, 512), BF16),
            pltpu.VMEM((2, ROWS, 512), BF16),
            pltpu.VMEM((2, N_ROW, CAP, 512), BF16),
            pltpu.VMEM((SLOTS, 512), F32),
            pltpu.VMEM((2, N_ROW, CAP, 512), BF16),
            pltpu.VMEM((N_ROW, 1, 128), I32),
            pltpu.VMEM((N_ROW, 1, 128), I32),
            pltpu.VMEM((N_ROW, 128), I32),
            pltpu.VMEM((512, 128), BF16),
            pltpu.VMEM((512, 128), BF16),
            pltpu.VMEM((512, 128), I32),
            pltpu.VMEM((SLOTS, 128), I32),
            pltpu.VMEM((SLOTS, ROWS), BF16),
            pltpu.VMEM((ROWS, 512), BF16),
            pltpu.VMEM((SLOTS, 512), BF16),
            dma((2,)), dma((2,)), dma((2,)), dma((N_ROW,)), dma((N_ROW,)), dma((2, N_ROW)), dma((2, N_ROW)),
        ],
        compiler_params=pltpu.CompilerParams(collective_id=0, has_side_effects=True, vmem_limit_bytes=VMEM),
        cost_estimate=pl.CostEstimate(flops=8 << 30, bytes_accessed=60 << 20, transcendentals=0),
        name="route",
    )(smap, part, bem)


def pack_kernel(j, a_piv, a_low, out, buf, isem, osem):
    me, col = lax.axis_index("row"), lax.axis_index("col")
    y, x, q = me // 8, (me // 2) % 4, col % 2
    ins = []
    for n, src in enumerate((a_piv, a_low)):
        for i in range(4):
            at = (1 - q) * (i * 4 + (x + j) % 4) + q * ((y + j) % 4 * 4 + i)
            ins.append(
                pltpu.make_async_copy(
                    src.at[:, pl.ds(pl.multiple_of(at * 512, 512), 512)], buf.at[n, i], isem.at[n, i]
                )
            )
            ins[-1].start()
    outs = []
    for n in range(2):
        for i in range(4):
            ins[n * 4 + i].wait()
            outs.append(pltpu.make_async_copy(buf.at[n, i], out.at[n, i], osem.at[n, i]))
            outs[-1].start()
    for copy in outs:
        copy.wait()


def pack(j, a_piv, a_low):
    hbm = pl.BlockSpec(memory_space=pl.ANY)
    return pl.pallas_call(
        functools.partial(pack_kernel, j),
        out_shape=jax.ShapeDtypeStruct((2, 4, 256, 512), BF16),
        in_specs=[hbm] * 2,
        out_specs=hbm,
        scratch_shapes=[
            pltpu.VMEM((2, 4, 256, 512), BF16),
            pltpu.SemaphoreType.DMA((2, 4)),
            pltpu.SemaphoreType.DMA((2, 4)),
        ],
        compiler_params=pltpu.CompilerParams(vmem_limit_bytes=VMEM),
        cost_estimate=pl.CostEstimate(flops=0, bytes_accessed=4 << 20, transcendentals=0),
        name="pack",
    )(a_piv, a_low)


def shift(v, j):
    pairs = []
    for r in range(N_ROW):
        y, x, z = r // 8, r // 2 % 4, r % 2
        for c in range(4):
            to = (y * 4 + (x + j) % 4) * 2 + z if c % 2 == 0 else ((y + j) % 4 * 4 + x) * 2 + z
            pairs.append((r * 4 + c, to * 4 + c))
    return lax.ppermute(v, ("row", "col"), pairs)


def panel_kernel(
    asm, a_piv, a_low, m1, m2, m3, out, tiles, b, acc, give, got,
    asem, zs, zr, gs, gr, fs, fr, ss, sr,
):
    me, col = lax.axis_index("row"), lax.axis_index("col")
    y, x, z, q = me // 8, (me // 2) % 4, me % 2, col % 2
    along = (1 - q) * y + q * x

    def on_gather(d):
        return (((y + (1 - q) * d) % 4) * 4 + (x + q * d) % 4) * 2 + z

    def on_scatter(d):
        return (((y + q * d) % 4) * 4 + (x + (1 - q) * d) % 4) * 2 + z

    other = me + 1 - 2 * z
    barrier = pltpu.get_barrier_semaphore()
    peers = [other] + [on_gather(d) for d in (1, 3, 2)] + [on_scatter(d) for d in (1, 3, 2)]
    for peer in peers:
        pl.semaphore_signal(barrier, inc=1, device_id=(peer, col), device_id_type=MESH)
    loads = []
    for n, own in enumerate((a_piv, a_low)):
        mine = []
        for i in range(4):
            at = (1 - q) * (i * 4 + x) + q * (y * 4 + i)
            mine.append(
                pltpu.make_async_copy(
                    own.at[:, pl.ds(pl.multiple_of(at * 512, 512), 512)], tiles.at[n, 0, i], asem.at[n, i]
                )
            )
        for j in range(3):
            mine.append(pltpu.make_async_copy((m1, m2, m3)[j].at[n], tiles.at[n, j + 1], asem.at[n, 4 + j]))
        for load in mine:
            load.start()
        loads.append(mine)

    sent = []

    def send(src, dst, s, r, to):
        copy = pltpu.make_async_remote_copy(src, dst, s, r, device_id=(to, col), device_id_type=MESH)
        copy.start()
        sent.append(copy)

    def hold(ref, s, r):
        pltpu.make_async_remote_copy(ref, ref, s, r, device_id=(other, col), device_id_type=MESH).wait_recv()

    def spot(d, dz):
        return (along + d) % 4 * 2 + (z + dz) % 2

    def first(n, h):
        ref = b.at[n, h, spot(0, 0)]
        send(ref, ref, zs.at[n, h], zr.at[n, h], other)
        for d in (1, 3, 2):
            send(ref, ref, gs.at[n, h, d], gr.at[n, h, d], on_gather(d))

    def relay(n, h):
        ref = b.at[n, h, spot(0, 1)]
        hold(ref, zs.at[n, h], zr.at[n, h])
        for d in (1, 3):
            send(ref, ref, fs.at[n, h, d], fr.at[n, h, d], on_gather(d))

    def near(n, h, d):
        ref = b.at[n, h, spot(d, 0)]
        hold(ref, gs.at[n, h, 4 - d], gr.at[n, h, 4 - d])
        if d == 2:
            send(ref, ref, fs.at[n, h, 2], fr.at[n, h, 2], other)

    def far(n, h, d):
        hold(b.at[n, h, spot(d, 1)], fs.at[n, h, 4 - d], fr.at[n, h, 4 - d])

    def piece(n, h, j, blocks):
        lhs = [
            tiles[n, j, (along + d) % 4, :, pl.ds(pl.multiple_of((z + dz) % 2 * 256, 256), 256)] for d, dz in blocks
        ]
        rhs = [b[n, h, spot(d, dz)] for d, dz in blocks]
        return jnp.dot(jnp.concatenate(lhs, axis=1), jnp.concatenate(rhs, axis=0), preferred_element_type=F32)

    def begin(n, h, *blocks):
        for j in range(4):
            acc[h, j] = piece(n, h, j, blocks)

    def add(n, h, *blocks):
        for j in range(4):
            acc[h, j] += piece(n, h, j, blocks)

    def last(n, h, *blocks):
        for j in (2, 1, 3):
            give[n, h, j] = (acc[h, j] + piece(n, h, j, blocks)).astype(BF16)
            send(give.at[n, h, j], got.at[n, h, j], ss.at[n, h, j], sr.at[n, h, j], on_scatter(4 - j))
        acc[h, 0] += piece(n, h, 0, blocks)

    def total(n, h):
        for j in (1, 3, 2):
            hold(got.at[n, h, j], ss.at[n, h, j], sr.at[n, h, j])
        return acc[h, 0] + (got[n, h, 1].astype(F32) + got[n, h, 3].astype(F32) + got[n, h, 2].astype(F32))

    def product(n):
        for load in loads[n]:
            load.wait()
        for h in range(2):
            near(n, h, 3)
            relay(n, h)
            near(n, h, 2)
            begin(n, h, (0, 0), (3, 0))
            near(n, h, 1)
            add(n, h, (0, 1), (1, 0))
        for h in range(2):
            far(n, h, 3)
            add(n, h, (2, 0), (3, 1))
            far(n, h, 1)
            far(n, h, 2)
            last(n, h, (1, 1), (2, 1))

    halves = [slice(h * 256, h * 256 + 256) for h in range(2)]
    for h in range(2):
        b[0, h, spot(0, 0)] = asm[0, :, halves[h]]
    pl.semaphore_wait(barrier, 7)
    for h in range(2):
        first(0, h)
    product(0)
    for h in range(2):
        solved = total(0, h).astype(BF16)
        b[1, h, spot(0, 0)] = solved
        first(1, h)
        out[0, :, halves[h]] = solved
    product(1)
    for h in range(2):
        out[1, :, halves[h]] = (asm[1, :, halves[h]].astype(F32) - total(1, h)).astype(BF16)
    for copy in sent:
        copy.wait_send()


def panel(asm, a_piv, a_low, moved):
    vm = pl.BlockSpec(memory_space=pltpu.VMEM)
    hbm = pl.BlockSpec(memory_space=pl.ANY)
    dma = pltpu.SemaphoreType.DMA
    return pl.pallas_call(
        panel_kernel,
        out_shape=jax.ShapeDtypeStruct((2, 256, 512), BF16),
        in_specs=[vm] + [hbm] * 5,
        out_specs=vm,
        scratch_shapes=[
            pltpu.VMEM((2, 4, 4, 256, 512), BF16),
            pltpu.VMEM((2, 2, 8, 256, 256), BF16),
            pltpu.VMEM((2, 4, 256, 256), F32),
            pltpu.VMEM((2, 2, 4, 256, 256), BF16),
            pltpu.VMEM((2, 2, 4, 256, 256), BF16),
            dma((2, 7)), dma((2, 2)), dma((2, 2)), dma((2, 2, 4)), dma((2, 2, 4)), dma((2, 2, 4)), dma((2, 2, 4)),
            dma((2, 2, 4)), dma((2, 2, 4)),
        ],
        compiler_params=pltpu.CompilerParams(collective_id=1, has_side_effects=True, vmem_limit_bytes=VMEM),
        cost_estimate=pl.CostEstimate(flops=4 << 30, bytes_accessed=64 << 20, transcendentals=0),
        name="panel",
    )(asm, a_piv, a_low, *moved)


def per_device(front_inverse, tiles, tile_row, tile_col, surface_map, bem, pivot, below):
    moved = {}
    for j in (1, 3, 2):
        moved[j] = shift(pack(j, pivot, below), j)
    moved = [moved[j] for j in (1, 2, 3)]
    part = front(tile_row, tile_col, front_inverse, tiles)
    asm = route(surface_map, part, bem)
    return panel(asm, pivot, below, moved)


def solution(mesh):
    placed = (
        P("row", "col"),
        P("col", None, None),
        P("col"),
        P("col"),
        P(None, "row"),
        P(None, "row", "col"),
        P("row", None),
        P("row", None),
    )
    return jax.shard_map(
        per_device, mesh=mesh, in_specs=placed, out_specs=P(None, "row", "col"), check_vma=False
    )
```

```python
import functools

import jax
import jax.numpy as jnp
from jax import lax
from jax.experimental import pallas as pl
from jax.experimental.pallas import tpu as pltpu
from jax.sharding import PartitionSpec as P

MESH = pl.DeviceIdType.MESH
F32, BF16, I32 = jnp.float32, jnp.bfloat16, jnp.int32
N_ROW, CAP = 32, 24
SLOTS = N_ROW * CAP
ROWS = 768
GROUP = 4
TILES = 192
PAIRS = 8
UNROLL = 5
CHUNKS = (TILES + PAIRS * (GROUP - 1)) // GROUP + UNROLL
VMEM = 63 << 20


def front_kernel(trow, tcol, f_hbm, t_hbm, out_hbm, f, w, acc, ob, cell, left, right, lrs, ccol, fsem, tsem, osem):
    loads = [
        pltpu.make_async_copy(t_hbm, w.at[pl.ds(0, TILES)], tsem),
        pltpu.make_async_copy(f_hbm, f, fsem),
    ]
    for load in loads:
        load.start()
    first = lax.axis_index("col") * 48

    @pl.loop(0, PAIRS * 12)
    def _(i):
        for u in range(8):
            cell[i * 8 + u] = TILES

    def fill(i, _):
        b = tcol[i]
        cell[(b // 2) * 96 + (trow[i] - first) * 2 + b % 2] = i
        return 0

    lax.fori_loop(0, TILES, fill, 0, unroll=8)

    def finish(n):
        for g in range(GROUP):
            left[n + g] = TILES
            right[n + g] = TILES
            lrs[n + g] = 0
        return (n + GROUP - 1) // GROUP * GROUP

    def place(b, n):
        def visit(lr, n):
            one, two = cell[b * 96 + lr * 2], cell[b * 96 + lr * 2 + 1]
            left[n], right[n], lrs[n] = one, two, lr
            return n + jnp.where(one + two == 2 * TILES, 0, 1)

        end = finish(lax.fori_loop(0, 48, visit, n, unroll=4))

        def name(c, _):
            ccol[c] = b
            return 0

        lax.fori_loop(n // GROUP, end // GROUP, name, 0)
        return end

    total = lax.fori_loop(0, PAIRS, place, 0) // GROUP
    for u in range(UNROLL - 1):
        finish((total + u) * GROUP)
        ccol[total + u] = 0
    w[TILES] = jnp.zeros((128, 128), BF16)
    acc[...] = jnp.zeros_like(acc)
    for load in loads:
        load.wait()

    @pl.loop(0, (total + UNROLL - 1) // UNROLL)
    def _(it):
        for u in range(UNROLL):
            c = it * UNROLL + u
            lhs, rhs = [], []
            for g in range(GROUP):
                k = c * GROUP + g
                lhs.append(f[:, pl.ds(pl.multiple_of(lrs[k] * 128, 128), 128)])
                rhs.append(jnp.concatenate([w[left[k]], w[right[k]]], axis=1))
            at = pl.multiple_of(ccol[c] * 256, 256)
            acc[:, pl.ds(at, 256)] += jnp.dot(
                jnp.concatenate(lhs, axis=1), jnp.concatenate(rhs, axis=0), preferred_element_type=F32
            )

    for k in range(4):
        ob[k] = acc[:, k * 512 : (k + 1) * 512].astype(BF16)
        pltpu.make_async_copy(ob.at[k], out_hbm.at[k], osem.at[k]).start()
    for k in range(4):
        pltpu.make_async_copy(ob.at[k], out_hbm.at[k], osem.at[k]).wait()


def front(trow, tcol, f, tiles):
    smem = pl.BlockSpec(memory_space=pltpu.SMEM)
    hbm = pl.BlockSpec(memory_space=pl.ANY)
    listed = pltpu.SMEM((CHUNKS * GROUP,), I32)
    return pl.pallas_call(
        front_kernel,
        out_shape=jax.ShapeDtypeStruct((4, ROWS, 512), BF16),
        in_specs=[smem, smem, hbm, hbm],
        out_specs=hbm,
        scratch_shapes=[
            pltpu.VMEM((ROWS, 6144), BF16),
            pltpu.VMEM((TILES + 1, 128, 128), BF16),
            pltpu.VMEM((ROWS, 2048), F32),
            pltpu.VMEM((4, ROWS, 512), BF16),
            pltpu.SMEM((PAIRS * 96,), I32),
            listed, listed, listed,
            pltpu.SMEM((CHUNKS,), I32),
            pltpu.SemaphoreType.DMA,
            pltpu.SemaphoreType.DMA,
            pltpu.SemaphoreType.DMA((4,)),
        ],
        compiler_params=pltpu.CompilerParams(vmem_limit_bytes=VMEM),
        cost_estimate=pl.CostEstimate(flops=20 << 30, bytes_accessed=60 << 20, transcendentals=0),
        name="front",
    )(trow, tcol, f, tiles)


def route_kernel(
    smap, part, bem, out, own, x, o, of, r, req, reqin, table, high, low, slotcol, cv, perm, sm, rb,
    os, ps, pr, rs, rr, sends, recvs,
):
    me, col = lax.axis_index("row"), lax.axis_index("col")
    q, lo = col % 2, col // 2
    barrier = pltpu.get_barrier_semaphore()

    def tell(a, b):
        pl.semaphore_signal(barrier, inc=1, device_id=(a, b), device_id_type=MESH)

    tell(me, lo * 2 + 1 - q)
    tell(me, (1 - lo) * 2 + q)

    @pl.loop(1, N_ROW)
    def _(p):
        for l in range(2):
            tell(lax.rem(me + p, N_ROW), l * 2 + q)

    mine = [pltpu.make_async_copy(part.at[l * 2 + q], own.at[l], os.at[l]) for l in range(2)]
    for copy in mine:
        copy.start()
    want = jnp.concatenate([smap[0:1, :], smap[1:2, :]], axis=1)
    owner = jnp.zeros_like(want)
    for k in range(1, N_ROW):
        owner += (want >= k * ROWS).astype(I32)
    local = want - owner * ROWS
    wide = want.shape[1]

    @pl.loop(0, wide // 64)
    def _(b):
        at = pl.ds(pl.multiple_of(b * 64, 64), 64)
        here = lax.broadcasted_iota(I32, (64, wide), 0) + b * 64
        lane = lax.broadcasted_iota(I32, (64, wide), 1)
        all_owner = jnp.broadcast_to(owner, (64, wide))
        own_col = jnp.sum(jnp.where(here == lane, all_owner, 0), axis=1, keepdims=True)
        value = jnp.sum(jnp.where(here == lane, jnp.broadcast_to(local, (64, wide)), 0), axis=1, keepdims=True) + 1
        before = jnp.where((own_col == all_owner) & (lane < here), 1, 0)
        rank = jnp.sum(before, axis=1, keepdims=True)
        slotcol[at, :] = jnp.broadcast_to(own_col * CAP + rank, (64, 128))
        hit = rank == lax.broadcasted_iota(I32, (64, 128), 1)
        high[at, :] = jnp.where(hit, value >> 5, 0).astype(F32).astype(BF16)
        low[at, :] = jnp.where(hit, value & 31, 0).astype(F32).astype(BF16)

    of_source = (jnp.broadcast_to(owner, (N_ROW, wide)) == lax.broadcasted_iota(I32, (N_ROW, wide), 0))
    of_source = of_source.astype(F32).astype(BF16)
    table[...] = (
        32.0 * jnp.dot(of_source, high[...], preferred_element_type=F32)
        + jnp.dot(of_source, low[...], preferred_element_type=F32)
    ).astype(I32) - 1

    @pl.loop(0, N_ROW)
    def _(s):
        req[s] = table[pl.ds(s, 1), :]

    pl.semaphore_wait(barrier, 64)

    def swap(l):
        return pltpu.make_async_remote_copy(
            part.at[l * 2 + 1 - q], x.at[l], ps.at[l], pr.at[l], device_id=(me, lo * 2 + 1 - q), device_id_type=MESH
        )

    def ask(s, who):
        return pltpu.make_async_remote_copy(
            req.at[s], reqin.at[who], rs.at[s], rr.at[who], device_id=(s, col), device_id_type=MESH
        )

    def give(l, d, who, wl):
        return pltpu.make_async_remote_copy(
            o.at[l, d], r.at[wl, who], sends.at[l, d], recvs.at[wl, who],
            device_id=(d, l * 2 + q), device_id_type=MESH,
        )

    swap(0).start()
    swap(1).start()

    @pl.loop(1, N_ROW)
    def _(p):
        ask(lax.rem(me + p, N_ROW), me).start()

    reqin[me] = req[me]
    for l in range(2):
        mine[l].wait()
        swap(l).wait_recv()
        sm[l] = (own[l].astype(F32) + x[l].astype(F32)).astype(BF16)

    @pl.loop(1, N_ROW)
    def _(p):
        s = lax.rem(me + p, N_ROW)
        ask(s, s).wait_recv()

    lane = lax.broadcasted_iota(I32, (CAP, 128), 1)
    line = lax.broadcasted_iota(I32, (CAP, 128), 0)

    @pl.loop(0, N_ROW)
    def _(d):
        row = jnp.broadcast_to(reqin[d], (CAP, 128))
        val = jnp.sum(jnp.where(lane == line, row, 0), axis=1, keepdims=True)
        cv[pl.ds(pl.multiple_of(d * CAP, 8), CAP), :] = jnp.broadcast_to(val, (CAP, 128))

    @pl.loop(0, SLOTS // 128)
    def _(b):
        at = pl.ds(pl.multiple_of(b * 128, 128), 128)
        want = cv[at, :]
        for j in range(ROWS // 128):
            here = lax.broadcasted_iota(I32, (128, 128), 1) + j * 128
            perm[at, j * 128 : (j + 1) * 128] = (want == here).astype(F32).astype(BF16)

    for l in range(2):
        of[...] = jnp.dot(perm[...], sm[l], preferred_element_type=F32)

        @pl.loop(0, N_ROW)
        def _(d):
            o[l, d] = of[pl.ds(pl.multiple_of(d * CAP, 8), CAP), :].astype(BF16)

        @pl.loop(1, N_ROW)
        def _(p):
            give(l, lax.rem(me + p, N_ROW), me, lo).start()

    give(1 - lo, me, me, lo).start()
    r[lo, me] = o[lo, me]
    give(lo, me, me, 1 - lo).wait_recv()
    of[pl.ds(pl.multiple_of(me * CAP, 8), CAP), :] = r[0, me].astype(F32) + r[1, me].astype(F32)

    @pl.loop(1, N_ROW)
    def _(p):
        s = lax.rem(me + N_ROW - p, N_ROW)
        for l in range(2):
            give(lo, s, s, l).wait_recv()
        of[pl.ds(pl.multiple_of(s * CAP, 8), CAP), :] = r[0, s].astype(F32) + r[1, s].astype(F32)

    rb[...] = of[...].astype(BF16)
    for p in range(2):
        pick = slotcol[p * 256 : (p + 1) * 256, :]
        sel = jnp.concatenate(
            [
                (pick == lax.broadcasted_iota(I32, (256, 128), 1) + j * 128).astype(F32).astype(BF16)
                for j in range(SLOTS // 128)
            ],
            axis=1,
        )
        schur = jnp.dot(sel, rb[...], preferred_element_type=F32)
        out[p] = (bem[p].astype(F32) - schur).astype(BF16)

    for l in range(2):
        swap(l).wait_send()
    give(1 - lo, me, me, lo).wait_send()

    @pl.loop(1, N_ROW)
    def _(p):
        d = lax.rem(me + p, N_ROW)
        ask(d, me).wait_send()
        for l in range(2):
            give(l, d, me, lo).wait_send()


def route(smap, part, bem):
    hbm = pl.BlockSpec(memory_space=pl.ANY)
    vm = pl.BlockSpec(memory_space=pltpu.VMEM)
    dma = pltpu.SemaphoreType.DMA
    return pl.pallas_call(
        route_kernel,
        out_shape=jax.ShapeDtypeStruct((2, 256, 512), BF16),
        in_specs=[vm, hbm, vm],
        out_specs=vm,
        scratch_shapes=[
            pltpu.VMEM((2, ROWS, 512), BF16),
            pltpu.VMEM((2, ROWS, 512), BF16),
            pltpu.VMEM((2, N_ROW, CAP, 512), BF16),
            pltpu.VMEM((SLOTS, 512), F32),
            pltpu.VMEM((2, N_ROW, CAP, 512), BF16),
            pltpu.VMEM((N_ROW, 1, 128), I32),
            pltpu.VMEM((N_ROW, 1, 128), I32),
            pltpu.VMEM((N_ROW, 128), I32),
            pltpu.VMEM((512, 128), BF16),
            pltpu.VMEM((512, 128), BF16),
            pltpu.VMEM((512, 128), I32),
            pltpu.VMEM((SLOTS, 128), I32),
            pltpu.VMEM((SLOTS, ROWS), BF16),
            pltpu.VMEM((2, ROWS, 512), BF16),
            pltpu.VMEM((SLOTS, 512), BF16),
            dma((2,)), dma((2,)), dma((2,)), dma((N_ROW,)), dma((N_ROW,)), dma((2, N_ROW)), dma((2, N_ROW)),
        ],
        compiler_params=pltpu.CompilerParams(collective_id=0, has_side_effects=True, vmem_limit_bytes=VMEM),
        cost_estimate=pl.CostEstimate(flops=8 << 30, bytes_accessed=60 << 20, transcendentals=0),
        name="route",
    )(smap, part, bem)


def pack_kernel(j, a_piv, a_low, out, buf, isem, osem):
    me, col = lax.axis_index("row"), lax.axis_index("col")
    y, x, q = me // 8, (me // 2) % 4, col % 2
    ins = []
    for n, src in enumerate((a_piv, a_low)):
        for i in range(4):
            at = (1 - q) * (i * 4 + (x + j) % 4) + q * ((y + j) % 4 * 4 + i)
            ins.append(
                pltpu.make_async_copy(
                    src.at[:, pl.ds(pl.multiple_of(at * 512, 512), 512)], buf.at[n, i], isem.at[n, i]
                )
            )
            ins[-1].start()
    outs = []
    for n in range(2):
        for i in range(4):
            ins[n * 4 + i].wait()
            outs.append(pltpu.make_async_copy(buf.at[n, i], out.at[n, i], osem.at[n, i]))
            outs[-1].start()
    for copy in outs:
        copy.wait()


def pack(j, a_piv, a_low):
    hbm = pl.BlockSpec(memory_space=pl.ANY)
    return pl.pallas_call(
        functools.partial(pack_kernel, j),
        out_shape=jax.ShapeDtypeStruct((2, 4, 256, 512), BF16),
        in_specs=[hbm] * 2,
        out_specs=hbm,
        scratch_shapes=[
            pltpu.VMEM((2, 4, 256, 512), BF16),
            pltpu.SemaphoreType.DMA((2, 4)),
            pltpu.SemaphoreType.DMA((2, 4)),
        ],
        compiler_params=pltpu.CompilerParams(vmem_limit_bytes=VMEM),
        cost_estimate=pl.CostEstimate(flops=0, bytes_accessed=4 << 20, transcendentals=0),
        name="pack",
    )(a_piv, a_low)


def start_kernel(a_piv, a_low, half, buf, isem, osem):
    me, col = lax.axis_index("row"), lax.axis_index("col")
    y, x, q, lo = me // 8, (me // 2) % 4, col % 2, col // 2

    def bring(src, i):
        at = (1 - q) * (i * 4 + (x + 2) % 4) + q * ((y + 2) % 4 * 4 + i)
        return pltpu.make_async_copy(
            src.at[:, pl.ds(pl.multiple_of(at * 512, 512), 512)], buf.at[i], isem.at[i]
        )

    @pl.when(lo == 0)
    def _():
        for i in range(4):
            bring(a_piv, i).start()

    @pl.when(lo == 1)
    def _():
        for i in range(4):
            bring(a_low, i).start()

    outs = []
    for i in range(4):
        bring(a_piv, i).wait()
        outs.append(pltpu.make_async_copy(buf.at[i], half.at[i], osem.at[i]))
        outs[-1].start()
    for copy in outs:
        copy.wait()


def start(a_piv, a_low):
    hbm = pl.BlockSpec(memory_space=pl.ANY)
    return pl.pallas_call(
        start_kernel,
        out_shape=jax.ShapeDtypeStruct((4, 256, 512), BF16),
        in_specs=[hbm] * 2,
        out_specs=hbm,
        scratch_shapes=[
            pltpu.VMEM((4, 256, 512), BF16),
            pltpu.SemaphoreType.DMA((4,)),
            pltpu.SemaphoreType.DMA((4,)),
        ],
        compiler_params=pltpu.CompilerParams(vmem_limit_bytes=VMEM),
        cost_estimate=pl.CostEstimate(flops=0, bytes_accessed=2 << 20, transcendentals=0),
        name="start",
    )(a_piv, a_low)


def shift(v, j):
    pairs = []
    for r in range(N_ROW):
        y, x, z = r // 8, r // 2 % 4, r % 2
        for c in range(4):
            to = (y * 4 + (x + j) % 4) * 2 + z if c % 2 == 0 else ((y + j) % 4 * 4 + x) * 2 + z
            pairs.append((r * 4 + c, to * 4 + c))
    return lax.ppermute(v, ("row", "col"), pairs)


def panel_kernel(
    asm, a_piv, a_low, m1, m3, half, twin, out, tiles, b, acc, give, got,
    asem, zs, zr, gs, gr, fs, fr, ss, sr,
):
    me, col = lax.axis_index("row"), lax.axis_index("col")
    y, x, z, q = me // 8, (me // 2) % 4, me % 2, col % 2
    along = (1 - q) * y + q * x

    def on_gather(d):
        return (((y + (1 - q) * d) % 4) * 4 + (x + q * d) % 4) * 2 + z

    def on_scatter(d):
        return (((y + q * d) % 4) * 4 + (x + (1 - q) * d) % 4) * 2 + z

    other = me + 1 - 2 * z
    barrier = pltpu.get_barrier_semaphore()
    peers = [other] + [on_gather(d) for d in (1, 3, 2)] + [on_scatter(d) for d in (1, 3, 2)]
    for peer in peers:
        pl.semaphore_signal(barrier, inc=1, device_id=(peer, col), device_id_type=MESH)
    loads = []
    for n, own in enumerate((a_piv, a_low)):
        mine = []
        for i in range(4):
            at = (1 - q) * (i * 4 + x) + q * (y * 4 + i)
            mine.append(
                pltpu.make_async_copy(
                    own.at[:, pl.ds(pl.multiple_of(at * 512, 512), 512)], tiles.at[n, 0, i], asem.at[n, i]
                )
            )
        for j, src in ((1, m1), (3, m3)):
            mine.append(pltpu.make_async_copy(src.at[n], tiles.at[n, j], asem.at[n, 3 + j]))
        for load in mine:
            load.start()
        mine.append(pltpu.make_async_copy(half, tiles.at[n, 2], asem.at[n, 5]))
        loads.append(mine)
    lo = col // 2
    pltpu.make_async_copy(half, tiles.at[lo, 2], asem.at[lo, 5]).start()
    pltpu.make_async_copy(twin, tiles.at[1 - lo, 2], asem.at[1 - lo, 5]).start()

    sent = []

    def send(src, dst, s, r, to):
        copy = pltpu.make_async_remote_copy(src, dst, s, r, device_id=(to, col), device_id_type=MESH)
        copy.start()
        sent.append(copy)

    def hold(ref, s, r):
        pltpu.make_async_remote_copy(ref, ref, s, r, device_id=(other, col), device_id_type=MESH).wait_recv()

    def spot(d, dz):
        return (along + d) % 4 * 2 + (z + dz) % 2

    def first(n, h):
        ref = b.at[n, h, spot(0, 0)]
        send(ref, ref, zs.at[n, h], zr.at[n, h], other)
        for d in (1, 3, 2):
            send(ref, ref, gs.at[n, h, d], gr.at[n, h, d], on_gather(d))

    def relay(n, h):
        ref = b.at[n, h, spot(0, 1)]
        hold(ref, zs.at[n, h], zr.at[n, h])
        for d in (1, 3):
            send(ref, ref, fs.at[n, h, d], fr.at[n, h, d], on_gather(d))

    def near(n, h, d):
        ref = b.at[n, h, spot(d, 0)]
        hold(ref, gs.at[n, h, 4 - d], gr.at[n, h, 4 - d])
        if d == 2:
            send(ref, ref, fs.at[n, h, 2], fr.at[n, h, 2], other)

    def far(n, h, d):
        hold(b.at[n, h, spot(d, 1)], fs.at[n, h, 4 - d], fr.at[n, h, 4 - d])

    def piece(n, h, j, blocks):
        lhs = [
            tiles[n, j, (along + d) % 4, :, pl.ds(pl.multiple_of((z + dz) % 2 * 256, 256), 256)] for d, dz in blocks
        ]
        rhs = [b[n, h, spot(d, dz)] for d, dz in blocks]
        return jnp.dot(jnp.concatenate(lhs, axis=1), jnp.concatenate(rhs, axis=0), preferred_element_type=F32)

    def begin(n, h, *blocks):
        for j in range(4):
            acc[h, j] = piece(n, h, j, blocks)

    def add(n, h, *blocks):
        for j in range(4):
            acc[h, j] += piece(n, h, j, blocks)

    def last(n, h, *blocks):
        for j in (2, 1, 3):
            give[n, h, j] = (acc[h, j] + piece(n, h, j, blocks)).astype(BF16)
            send(give.at[n, h, j], got.at[n, h, j], ss.at[n, h, j], sr.at[n, h, j], on_scatter(4 - j))
        acc[h, 0] += piece(n, h, 0, blocks)

    def total(n, h):
        for j in (1, 3, 2):
            hold(got.at[n, h, j], ss.at[n, h, j], sr.at[n, h, j])
        return acc[h, 0] + (got[n, h, 1].astype(F32) + got[n, h, 3].astype(F32) + got[n, h, 2].astype(F32))

    def product(n):
        for load in loads[n]:
            load.wait()
        for h in range(2):
            near(n, h, 3)
            relay(n, h)
            near(n, h, 2)
            begin(n, h, (0, 0), (3, 0))
            near(n, h, 1)
            add(n, h, (0, 1), (1, 0))
        for h in range(2):
            far(n, h, 3)
            add(n, h, (2, 0), (3, 1))
            far(n, h, 1)
            far(n, h, 2)
            last(n, h, (1, 1), (2, 1))

    halves = [slice(h * 256, h * 256 + 256) for h in range(2)]
    for h in range(2):
        b[0, h, spot(0, 0)] = asm[0, :, halves[h]]
    pl.semaphore_wait(barrier, 7)
    for h in range(2):
        first(0, h)
    product(0)
    for h in range(2):
        solved = total(0, h).astype(BF16)
        b[1, h, spot(0, 0)] = solved
        first(1, h)
        out[0, :, halves[h]] = solved
    product(1)
    for h in range(2):
        out[1, :, halves[h]] = (asm[1, :, halves[h]].astype(F32) - total(1, h)).astype(BF16)
    for copy in sent:
        copy.wait_send()


def panel(asm, a_piv, a_low, moved):
    vm = pl.BlockSpec(memory_space=pltpu.VMEM)
    hbm = pl.BlockSpec(memory_space=pl.ANY)
    dma = pltpu.SemaphoreType.DMA
    return pl.pallas_call(
        panel_kernel,
        out_shape=jax.ShapeDtypeStruct((2, 256, 512), BF16),
        in_specs=[vm] + [hbm] * 6,
        out_specs=vm,
        scratch_shapes=[
            pltpu.VMEM((2, 4, 4, 256, 512), BF16),
            pltpu.VMEM((2, 2, 8, 256, 256), BF16),
            pltpu.VMEM((2, 4, 256, 256), F32),
            pltpu.VMEM((2, 2, 4, 256, 256), BF16),
            pltpu.VMEM((2, 2, 4, 256, 256), BF16),
            dma((2, 7)), dma((2, 2)), dma((2, 2)), dma((2, 2, 4)), dma((2, 2, 4)), dma((2, 2, 4)), dma((2, 2, 4)),
            dma((2, 2, 4)), dma((2, 2, 4)),
        ],
        compiler_params=pltpu.CompilerParams(collective_id=1, has_side_effects=True, vmem_limit_bytes=VMEM),
        cost_estimate=pl.CostEstimate(flops=4 << 30, bytes_accessed=64 << 20, transcendentals=0),
        name="panel",
    )(asm, a_piv, a_low, *moved)


def per_device(front_inverse, tiles, tile_row, tile_col, surface_map, bem, pivot, below):
    half = shift(start(pivot, below), 2)
    m1 = shift(pack(1, pivot, below), 1)
    m3 = shift(pack(3, pivot, below), 3)
    half, tile_row = lax.optimization_barrier((half, tile_row))
    twin = lax.ppermute(half, "col", [(c, (c + 2) % 4) for c in range(4)])
    part = front(tile_row, tile_col, front_inverse, tiles)
    asm = route(surface_map, part, bem)
    return panel(asm, pivot, below, (m1, m3, half, twin))


def solution(mesh):
    placed = (
        P("row", "col"),
        P("col", None, None),
        P("col"),
        P("col"),
        P(None, "row"),
        P(None, "row", "col"),
        P("row", None),
        P("row", None),
    )
    return jax.shard_map(
        per_device, mesh=mesh, in_specs=placed, out_specs=P(None, "row", "col"), check_vma=False
    )
```

```python
import functools

import jax
import jax.numpy as jnp
from jax import lax
from jax.experimental import pallas as pl
from jax.experimental.pallas import tpu as pltpu
from jax.sharding import PartitionSpec as P

MESH = pl.DeviceIdType.MESH
F32, BF16, I32 = jnp.float32, jnp.bfloat16, jnp.int32
N_ROW, CAP = 32, 24
SLOTS = N_ROW * CAP
ROWS = 768
GROUP = 4
TILES = 192
PAIRS = 8
UNROLL = 5
CHUNKS = (TILES + PAIRS * (GROUP - 1)) // GROUP + UNROLL
VMEM = 63 << 20


def front_kernel(trow, tcol, f_hbm, t_hbm, out_hbm, f, w, acc, ob, cell, left, right, lrs, ccol, fsem, tsem, osem):
    loads = [
        pltpu.make_async_copy(t_hbm, w.at[pl.ds(0, TILES)], tsem),
        pltpu.make_async_copy(f_hbm, f, fsem),
    ]
    for load in loads:
        load.start()
    first = lax.axis_index("col") * 48

    @pl.loop(0, PAIRS * 12)
    def _(i):
        for u in range(8):
            cell[i * 8 + u] = TILES

    def fill(i, _):
        b = tcol[i]
        cell[(b // 2) * 96 + (trow[i] - first) * 2 + b % 2] = i
        return 0

    lax.fori_loop(0, TILES, fill, 0, unroll=8)

    def finish(n):
        for g in range(GROUP):
            left[n + g] = TILES
            right[n + g] = TILES
            lrs[n + g] = 0
        return (n + GROUP - 1) // GROUP * GROUP

    def place(b, n):
        def visit(lr, n):
            one, two = cell[b * 96 + lr * 2], cell[b * 96 + lr * 2 + 1]
            left[n], right[n], lrs[n] = one, two, lr
            return n + jnp.where(one + two == 2 * TILES, 0, 1)

        end = finish(lax.fori_loop(0, 48, visit, n, unroll=4))

        def name(c, _):
            ccol[c] = b
            return 0

        lax.fori_loop(n // GROUP, end // GROUP, name, 0)
        return end

    total = lax.fori_loop(0, PAIRS, place, 0) // GROUP
    for u in range(UNROLL - 1):
        finish((total + u) * GROUP)
        ccol[total + u] = 0
    w[TILES] = jnp.zeros((128, 128), BF16)
    acc[...] = jnp.zeros_like(acc)
    for load in loads:
        load.wait()

    @pl.loop(0, (total + UNROLL - 1) // UNROLL)
    def _(it):
        for u in range(UNROLL):
            c = it * UNROLL + u
            lhs, rhs = [], []
            for g in range(GROUP):
                k = c * GROUP + g
                lhs.append(f[:, pl.ds(pl.multiple_of(lrs[k] * 128, 128), 128)])
                rhs.append(jnp.concatenate([w[left[k]], w[right[k]]], axis=1))
            at = pl.multiple_of(ccol[c] * 256, 256)
            acc[:, pl.ds(at, 256)] += jnp.dot(
                jnp.concatenate(lhs, axis=1), jnp.concatenate(rhs, axis=0), preferred_element_type=F32
            )

    for k in range(4):
        ob[k] = acc[:, k * 512 : (k + 1) * 512].astype(BF16)
        pltpu.make_async_copy(ob.at[k], out_hbm.at[k], osem.at[k]).start()
    for k in range(4):
        pltpu.make_async_copy(ob.at[k], out_hbm.at[k], osem.at[k]).wait()


def front(trow, tcol, f, tiles):
    smem = pl.BlockSpec(memory_space=pltpu.SMEM)
    hbm = pl.BlockSpec(memory_space=pl.ANY)
    listed = pltpu.SMEM((CHUNKS * GROUP,), I32)
    return pl.pallas_call(
        front_kernel,
        out_shape=jax.ShapeDtypeStruct((4, ROWS, 512), BF16),
        in_specs=[smem, smem, hbm, hbm],
        out_specs=hbm,
        scratch_shapes=[
            pltpu.VMEM((ROWS, 6144), BF16),
            pltpu.VMEM((TILES + 1, 128, 128), BF16),
            pltpu.VMEM((ROWS, 2048), F32),
            pltpu.VMEM((4, ROWS, 512), BF16),
            pltpu.SMEM((PAIRS * 96,), I32),
            listed, listed, listed,
            pltpu.SMEM((CHUNKS,), I32),
            pltpu.SemaphoreType.DMA,
            pltpu.SemaphoreType.DMA,
            pltpu.SemaphoreType.DMA((4,)),
        ],
        compiler_params=pltpu.CompilerParams(vmem_limit_bytes=VMEM),
        cost_estimate=pl.CostEstimate(flops=20 << 30, bytes_accessed=60 << 20, transcendentals=0),
        name="front",
    )(trow, tcol, f, tiles)


def route_kernel(
    smap, part, bem, own, x, o, of, r, req, reqin, table, high, low, slotcol, cv, perm, sm, rb,
    os, ps, pr, rs, rr, sends, recvs,
):
    me, col = lax.axis_index("row"), lax.axis_index("col")
    q, lo = col % 2, col // 2
    barrier = pltpu.get_barrier_semaphore()

    def tell(a, b):
        pl.semaphore_signal(barrier, inc=1, device_id=(a, b), device_id_type=MESH)

    tell(me, lo * 2 + 1 - q)
    tell(me, (1 - lo) * 2 + q)

    @pl.loop(1, N_ROW)
    def _(p):
        for l in range(2):
            tell(lax.rem(me + p, N_ROW), l * 2 + q)

    mine = [pltpu.make_async_copy(part.at[l * 2 + q], own.at[l], os.at[l]) for l in range(2)]
    for copy in mine:
        copy.start()
    want = jnp.concatenate([smap[0:1, :], smap[1:2, :]], axis=1)
    owner = jnp.zeros_like(want)
    for k in range(1, N_ROW):
        owner += (want >= k * ROWS).astype(I32)
    local = want - owner * ROWS
    wide = want.shape[1]

    @pl.loop(0, wide // 64)
    def _(b):
        at = pl.ds(pl.multiple_of(b * 64, 64), 64)
        here = lax.broadcasted_iota(I32, (64, wide), 0) + b * 64
        lane = lax.broadcasted_iota(I32, (64, wide), 1)
        all_owner = jnp.broadcast_to(owner, (64, wide))
        own_col = jnp.sum(jnp.where(here == lane, all_owner, 0), axis=1, keepdims=True)
        value = jnp.sum(jnp.where(here == lane, jnp.broadcast_to(local, (64, wide)), 0), axis=1, keepdims=True) + 1
        before = jnp.where((own_col == all_owner) & (lane < here), 1, 0)
        rank = jnp.sum(before, axis=1, keepdims=True)
        slotcol[at, :] = jnp.broadcast_to(own_col * CAP + rank, (64, 128))
        hit = rank == lax.broadcasted_iota(I32, (64, 128), 1)
        high[at, :] = jnp.where(hit, value >> 5, 0).astype(F32).astype(BF16)
        low[at, :] = jnp.where(hit, value & 31, 0).astype(F32).astype(BF16)

    of_source = (jnp.broadcast_to(owner, (N_ROW, wide)) == lax.broadcasted_iota(I32, (N_ROW, wide), 0))
    of_source = of_source.astype(F32).astype(BF16)
    table[...] = (
        32.0 * jnp.dot(of_source, high[...], preferred_element_type=F32)
        + jnp.dot(of_source, low[...], preferred_element_type=F32)
    ).astype(I32) - 1

    @pl.loop(0, N_ROW)
    def _(s):
        req[s] = table[pl.ds(s, 1), :]

    pl.semaphore_wait(barrier, 64)

    def swap(l):
        return pltpu.make_async_remote_copy(
            part.at[l * 2 + 1 - q], x.at[l], ps.at[l], pr.at[l], device_id=(me, lo * 2 + 1 - q), device_id_type=MESH
        )

    def ask(s, who):
        return pltpu.make_async_remote_copy(
            req.at[s], reqin.at[who], rs.at[s], rr.at[who], device_id=(s, col), device_id_type=MESH
        )

    def give(l, d, who, wl):
        return pltpu.make_async_remote_copy(
            o.at[l, d], r.at[wl, who], sends.at[l, d], recvs.at[wl, who],
            device_id=(d, l * 2 + q), device_id_type=MESH,
        )

    swap(0).start()
    swap(1).start()

    @pl.loop(1, N_ROW)
    def _(p):
        ask(lax.rem(me + p, N_ROW), me).start()

    reqin[me] = req[me]
    for l in range(2):
        mine[l].wait()
        swap(l).wait_recv()
        sm[l] = (own[l].astype(F32) + x[l].astype(F32)).astype(BF16)

    @pl.loop(1, N_ROW)
    def _(p):
        s = lax.rem(me + p, N_ROW)
        ask(s, s).wait_recv()

    lane = lax.broadcasted_iota(I32, (CAP, 128), 1)
    line = lax.broadcasted_iota(I32, (CAP, 128), 0)

    @pl.loop(0, N_ROW)
    def _(d):
        row = jnp.broadcast_to(reqin[d], (CAP, 128))
        val = jnp.sum(jnp.where(lane == line, row, 0), axis=1, keepdims=True)
        cv[pl.ds(pl.multiple_of(d * CAP, 8), CAP), :] = jnp.broadcast_to(val, (CAP, 128))

    @pl.loop(0, SLOTS // 128)
    def _(b):
        at = pl.ds(pl.multiple_of(b * 128, 128), 128)
        want = cv[at, :]
        for j in range(ROWS // 128):
            here = lax.broadcasted_iota(I32, (128, 128), 1) + j * 128
            perm[at, j * 128 : (j + 1) * 128] = (want == here).astype(F32).astype(BF16)

    for l in range(2):
        of[...] = jnp.dot(perm[...], sm[l], preferred_element_type=F32)

        @pl.loop(0, N_ROW)
        def _(d):
            o[l, d] = of[pl.ds(pl.multiple_of(d * CAP, 8), CAP), :].astype(BF16)

        @pl.loop(1, N_ROW)
        def _(p):
            give(l, lax.rem(me + p, N_ROW), me, lo).start()

    give(1 - lo, me, me, lo).start()
    r[lo, me] = o[lo, me]
    give(lo, me, me, 1 - lo).wait_recv()
    of[pl.ds(pl.multiple_of(me * CAP, 8), CAP), :] = r[0, me].astype(F32) + r[1, me].astype(F32)

    @pl.loop(1, N_ROW)
    def _(p):
        s = lax.rem(me + N_ROW - p, N_ROW)
        for l in range(2):
            give(lo, s, s, l).wait_recv()
        of[pl.ds(pl.multiple_of(s * CAP, 8), CAP), :] = r[0, s].astype(F32) + r[1, s].astype(F32)

    rb[...] = of[...].astype(BF16)

    def assembled(p):
        pick = slotcol[p * 256 : (p + 1) * 256, :]
        sel = jnp.concatenate(
            [
                (pick == lax.broadcasted_iota(I32, (256, 128), 1) + j * 128).astype(F32).astype(BF16)
                for j in range(SLOTS // 128)
            ],
            axis=1,
        )
        schur = jnp.dot(sel, rb[...], preferred_element_type=F32)
        return (bem[p].astype(F32) - schur).astype(BF16)

    def finish():
        for l in range(2):
            swap(l).wait_send()
        give(1 - lo, me, me, lo).wait_send()

        @pl.loop(1, N_ROW)
        def _(p):
            d = lax.rem(me + p, N_ROW)
            ask(d, me).wait_send()
            for l in range(2):
                give(l, d, me, lo).wait_send()

    return assembled, finish


def pack_kernel(j, a_piv, a_low, out, buf, isem, osem):
    me, col = lax.axis_index("row"), lax.axis_index("col")
    y, x, q = me // 8, (me // 2) % 4, col % 2
    ins = []
    for n, src in enumerate((a_piv, a_low)):
        for i in range(4):
            at = (1 - q) * (i * 4 + (x + j) % 4) + q * ((y + j) % 4 * 4 + i)
            ins.append(
                pltpu.make_async_copy(
                    src.at[:, pl.ds(pl.multiple_of(at * 512, 512), 512)], buf.at[n, i], isem.at[n, i]
                )
            )
            ins[-1].start()
    outs = []
    for n in range(2):
        for i in range(4):
            ins[n * 4 + i].wait()
            outs.append(pltpu.make_async_copy(buf.at[n, i], out.at[n, i], osem.at[n, i]))
            outs[-1].start()
    for copy in outs:
        copy.wait()


def pack(j, a_piv, a_low):
    hbm = pl.BlockSpec(memory_space=pl.ANY)
    return pl.pallas_call(
        functools.partial(pack_kernel, j),
        out_shape=jax.ShapeDtypeStruct((2, 4, 256, 512), BF16),
        in_specs=[hbm] * 2,
        out_specs=hbm,
        scratch_shapes=[
            pltpu.VMEM((2, 4, 256, 512), BF16),
            pltpu.SemaphoreType.DMA((2, 4)),
            pltpu.SemaphoreType.DMA((2, 4)),
        ],
        compiler_params=pltpu.CompilerParams(vmem_limit_bytes=VMEM),
        cost_estimate=pl.CostEstimate(flops=0, bytes_accessed=4 << 20, transcendentals=0),
        name="pack",
    )(a_piv, a_low)


def start_kernel(a_piv, a_low, half, buf, isem, osem):
    me, col = lax.axis_index("row"), lax.axis_index("col")
    y, x, q, lo = me // 8, (me // 2) % 4, col % 2, col // 2

    def bring(src, i):
        at = (1 - q) * (i * 4 + (x + 2) % 4) + q * ((y + 2) % 4 * 4 + i)
        return pltpu.make_async_copy(
            src.at[:, pl.ds(pl.multiple_of(at * 512, 512), 512)], buf.at[i], isem.at[i]
        )

    @pl.when(lo == 0)
    def _():
        for i in range(4):
            bring(a_piv, i).start()

    @pl.when(lo == 1)
    def _():
        for i in range(4):
            bring(a_low, i).start()

    outs = []
    for i in range(4):
        bring(a_piv, i).wait()
        outs.append(pltpu.make_async_copy(buf.at[i], half.at[i], osem.at[i]))
        outs[-1].start()
    for copy in outs:
        copy.wait()


def start(a_piv, a_low):
    hbm = pl.BlockSpec(memory_space=pl.ANY)
    return pl.pallas_call(
        start_kernel,
        out_shape=jax.ShapeDtypeStruct((4, 256, 512), BF16),
        in_specs=[hbm] * 2,
        out_specs=hbm,
        scratch_shapes=[
            pltpu.VMEM((4, 256, 512), BF16),
            pltpu.SemaphoreType.DMA((4,)),
            pltpu.SemaphoreType.DMA((4,)),
        ],
        compiler_params=pltpu.CompilerParams(vmem_limit_bytes=VMEM),
        cost_estimate=pl.CostEstimate(flops=0, bytes_accessed=2 << 20, transcendentals=0),
        name="start",
    )(a_piv, a_low)


def shift(v, j):
    pairs = []
    for r in range(N_ROW):
        y, x, z = r // 8, r // 2 % 4, r % 2
        for c in range(4):
            to = (y * 4 + (x + j) % 4) * 2 + z if c % 2 == 0 else ((y + j) % 4 * 4 + x) * 2 + z
            pairs.append((r * 4 + c, to * 4 + c))
    return lax.ppermute(v, ("row", "col"), pairs)


def panel_kernel(
    a_piv, a_low, m1, m3, half, twin, out, keep, tiles, b, acc, give, got,
    asem, zs, zr, gs, gr, fs, fr, ss, sr,
):
    me, col = lax.axis_index("row"), lax.axis_index("col")
    y, x, z, q = me // 8, (me // 2) % 4, me % 2, col % 2
    along = (1 - q) * y + q * x

    def on_gather(d):
        return (((y + (1 - q) * d) % 4) * 4 + (x + q * d) % 4) * 2 + z

    def on_scatter(d):
        return (((y + q * d) % 4) * 4 + (x + (1 - q) * d) % 4) * 2 + z

    other = me + 1 - 2 * z
    loads = []
    for n, own in enumerate((a_piv, a_low)):
        mine = []
        for i in range(4):
            at = (1 - q) * (i * 4 + x) + q * (y * 4 + i)
            mine.append(
                pltpu.make_async_copy(
                    own.at[:, pl.ds(pl.multiple_of(at * 512, 512), 512)], tiles.at[n, 0, i], asem.at[n, i]
                )
            )
        for j, src in ((1, m1), (3, m3)):
            mine.append(pltpu.make_async_copy(src.at[n], tiles.at[n, j], asem.at[n, 3 + j]))
        for load in mine:
            load.start()
        mine.append(pltpu.make_async_copy(half, tiles.at[n, 2], asem.at[n, 5]))
        loads.append(mine)
    lo = col // 2
    pltpu.make_async_copy(half, tiles.at[lo, 2], asem.at[lo, 5]).start()
    pltpu.make_async_copy(twin, tiles.at[1 - lo, 2], asem.at[1 - lo, 5]).start()

    sent = []

    def send(src, dst, s, r, to):
        copy = pltpu.make_async_remote_copy(src, dst, s, r, device_id=(to, col), device_id_type=MESH)
        copy.start()
        sent.append(copy)

    def hold(ref, s, r):
        pltpu.make_async_remote_copy(ref, ref, s, r, device_id=(other, col), device_id_type=MESH).wait_recv()

    def spot(d, dz):
        return (along + d) % 4 * 2 + (z + dz) % 2

    def first(n, h):
        ref = b.at[n, h, spot(0, 0)]
        send(ref, ref, zs.at[n, h], zr.at[n, h], other)
        for d in (1, 3, 2):
            send(ref, ref, gs.at[n, h, d], gr.at[n, h, d], on_gather(d))

    def relay(n, h):
        ref = b.at[n, h, spot(0, 1)]
        hold(ref, zs.at[n, h], zr.at[n, h])
        for d in (1, 3):
            send(ref, ref, fs.at[n, h, d], fr.at[n, h, d], on_gather(d))

    def near(n, h, d):
        ref = b.at[n, h, spot(d, 0)]
        hold(ref, gs.at[n, h, 4 - d], gr.at[n, h, 4 - d])
        if d == 2:
            send(ref, ref, fs.at[n, h, 2], fr.at[n, h, 2], other)

    def far(n, h, d):
        hold(b.at[n, h, spot(d, 1)], fs.at[n, h, 4 - d], fr.at[n, h, 4 - d])

    def piece(n, h, j, blocks):
        lhs = [
            tiles[n, j, (along + d) % 4, :, pl.ds(pl.multiple_of((z + dz) % 2 * 256, 256), 256)] for d, dz in blocks
        ]
        rhs = [b[n, h, spot(d, dz)] for d, dz in blocks]
        return jnp.dot(jnp.concatenate(lhs, axis=1), jnp.concatenate(rhs, axis=0), preferred_element_type=F32)

    def begin(n, h, *blocks):
        for j in range(4):
            acc[h, j] = piece(n, h, j, blocks)

    def add(n, h, *blocks):
        for j in range(4):
            acc[h, j] += piece(n, h, j, blocks)

    def last(n, h, *blocks):
        for j in (2, 1, 3):
            give[n, h, j] = (acc[h, j] + piece(n, h, j, blocks)).astype(BF16)
            send(give.at[n, h, j], got.at[n, h, j], ss.at[n, h, j], sr.at[n, h, j], on_scatter(4 - j))
        acc[h, 0] += piece(n, h, 0, blocks)

    def total(n, h):
        for j in (1, 3, 2):
            hold(got.at[n, h, j], ss.at[n, h, j], sr.at[n, h, j])
        return acc[h, 0] + (got[n, h, 1].astype(F32) + got[n, h, 3].astype(F32) + got[n, h, 2].astype(F32))

    def product(n):
        for load in loads[n]:
            load.wait()
        for h in range(2):
            near(n, h, 3)
            relay(n, h)
            near(n, h, 2)
            begin(n, h, (0, 0), (3, 0))
            near(n, h, 1)
            add(n, h, (0, 1), (1, 0))
        for h in range(2):
            far(n, h, 3)
            add(n, h, (2, 0), (3, 1))
            far(n, h, 1)
            far(n, h, 2)
            last(n, h, (1, 1), (2, 1))

    halves = [slice(h * 256, h * 256 + 256) for h in range(2)]

    def run(assembled):
        block = assembled(0)
        for h in range(2):
            b[0, h, spot(0, 0)] = block[:, halves[h]]
        for h in range(2):
            first(0, h)
        keep[...] = assembled(1)
        product(0)
        for h in range(2):
            solved = total(0, h).astype(BF16)
            b[1, h, spot(0, 0)] = solved
            first(1, h)
            out[0, :, halves[h]] = solved
        product(1)
        for h in range(2):
            out[1, :, halves[h]] = (keep[:, halves[h]].astype(F32) - total(1, h)).astype(BF16)
        for copy in sent:
            copy.wait_send()

    return run


ROUTE_REFS = 22


def tail_kernel(smap, part, bem, a_piv, a_low, m1, m3, half, twin, out, *refs):
    run = panel_kernel(a_piv, a_low, m1, m3, half, twin, out, *refs[ROUTE_REFS:])
    assembled, finish = route_kernel(smap, part, bem, *refs[:ROUTE_REFS])
    run(assembled)
    finish()


def tail(smap, part, bem, a_piv, a_low, moved):
    vm = pl.BlockSpec(memory_space=pltpu.VMEM)
    hbm = pl.BlockSpec(memory_space=pl.ANY)
    dma = pltpu.SemaphoreType.DMA
    return pl.pallas_call(
        tail_kernel,
        out_shape=jax.ShapeDtypeStruct((2, 256, 512), BF16),
        in_specs=[vm, hbm, vm] + [hbm] * 6,
        out_specs=vm,
        scratch_shapes=[
            pltpu.VMEM((2, ROWS, 512), BF16),
            pltpu.VMEM((2, ROWS, 512), BF16),
            pltpu.VMEM((2, N_ROW, CAP, 512), BF16),
            pltpu.VMEM((SLOTS, 512), F32),
            pltpu.VMEM((2, N_ROW, CAP, 512), BF16),
            pltpu.VMEM((N_ROW, 1, 128), I32),
            pltpu.VMEM((N_ROW, 1, 128), I32),
            pltpu.VMEM((N_ROW, 128), I32),
            pltpu.VMEM((512, 128), BF16),
            pltpu.VMEM((512, 128), BF16),
            pltpu.VMEM((512, 128), I32),
            pltpu.VMEM((SLOTS, 128), I32),
            pltpu.VMEM((SLOTS, ROWS), BF16),
            pltpu.VMEM((2, ROWS, 512), BF16),
            pltpu.VMEM((SLOTS, 512), BF16),
            dma((2,)), dma((2,)), dma((2,)), dma((N_ROW,)), dma((N_ROW,)), dma((2, N_ROW)), dma((2, N_ROW)),
            pltpu.VMEM((256, 512), BF16),
            pltpu.VMEM((2, 4, 4, 256, 512), BF16),
            pltpu.VMEM((2, 2, 8, 256, 256), BF16),
            pltpu.VMEM((2, 4, 256, 256), F32),
            pltpu.VMEM((2, 2, 4, 256, 256), BF16),
            pltpu.VMEM((2, 2, 4, 256, 256), BF16),
            dma((2, 7)), dma((2, 2)), dma((2, 2)), dma((2, 2, 4)), dma((2, 2, 4)), dma((2, 2, 4)), dma((2, 2, 4)),
            dma((2, 2, 4)), dma((2, 2, 4)),
        ],
        compiler_params=pltpu.CompilerParams(collective_id=0, has_side_effects=True, vmem_limit_bytes=VMEM),
        cost_estimate=pl.CostEstimate(flops=12 << 30, bytes_accessed=120 << 20, transcendentals=0),
        name="tail",
    )(smap, part, bem, a_piv, a_low, *moved)


def per_device(front_inverse, tiles, tile_row, tile_col, surface_map, bem, pivot, below):
    half = shift(start(pivot, below), 2)
    m1, m3 = pack(1, pivot, below), pack(3, pivot, below)
    half, m1, m3, tile_row = lax.optimization_barrier((half, m1, m3, tile_row))
    twin = lax.ppermute(half, "col", [(c, (c + 2) % 4) for c in range(4)])
    m1, m3 = shift(m1, 1), shift(m3, 3)
    part = front(tile_row, tile_col, front_inverse, tiles)
    return tail(surface_map, part, bem, pivot, below, (m1, m3, half, twin))


def solution(mesh):
    placed = (
        P("row", "col"),
        P("col", None, None),
        P("col"),
        P("col"),
        P(None, "row"),
        P(None, "row", "col"),
        P("row", None),
        P("row", None),
    )
    return jax.shard_map(
        per_device, mesh=mesh, in_specs=placed, out_specs=P(None, "row", "col"), check_vma=False
    )
```

```python
import functools

import jax
import jax.numpy as jnp
from jax import lax
from jax.experimental import pallas as pl
from jax.experimental.pallas import tpu as pltpu
from jax.sharding import PartitionSpec as P

MESH = pl.DeviceIdType.MESH
F32, BF16, I32 = jnp.float32, jnp.bfloat16, jnp.int32
N_ROW, CAP = 32, 24
SLOTS = N_ROW * CAP
ROWS = 768
GROUP = 4
TILES = 192
PAIRS = 8
UNROLL = 5
CHUNKS = (TILES + PAIRS * (GROUP - 1)) // GROUP + UNROLL
VMEM = 63 << 20


def front_kernel(trow, tcol, f_hbm, t_hbm, out_hbm, f, w, acc, ob, cell, left, right, lrs, ccol, fsem, tsem, osem):
    loads = [
        pltpu.make_async_copy(t_hbm, w.at[pl.ds(0, TILES)], tsem),
        pltpu.make_async_copy(f_hbm, f, fsem),
    ]
    for load in loads:
        load.start()
    first = lax.axis_index("col") * 48

    @pl.loop(0, PAIRS * 12)
    def _(i):
        for u in range(8):
            cell[i * 8 + u] = TILES

    def fill(i, _):
        b = tcol[i]
        cell[(b // 2) * 96 + (trow[i] - first) * 2 + b % 2] = i
        return 0

    lax.fori_loop(0, TILES, fill, 0, unroll=8)

    def finish(n):
        for g in range(GROUP):
            left[n + g] = TILES
            right[n + g] = TILES
            lrs[n + g] = 0
        return (n + GROUP - 1) // GROUP * GROUP

    def place(b, n):
        def visit(lr, n):
            one, two = cell[b * 96 + lr * 2], cell[b * 96 + lr * 2 + 1]
            left[n], right[n], lrs[n] = one, two, lr
            return n + jnp.where(one + two == 2 * TILES, 0, 1)

        end = finish(lax.fori_loop(0, 48, visit, n, unroll=4))

        def name(c, _):
            ccol[c] = b
            return 0

        lax.fori_loop(n // GROUP, end // GROUP, name, 0)
        return end

    total = lax.fori_loop(0, PAIRS, place, 0) // GROUP
    for u in range(UNROLL - 1):
        finish((total + u) * GROUP)
        ccol[total + u] = 0
    w[TILES] = jnp.zeros((128, 128), BF16)
    acc[...] = jnp.zeros_like(acc)
    for load in loads:
        load.wait()

    @pl.loop(0, (total + UNROLL - 1) // UNROLL)
    def _(it):
        for u in range(UNROLL):
            c = it * UNROLL + u
            lhs, rhs = [], []
            for g in range(GROUP):
                k = c * GROUP + g
                lhs.append(f[:, pl.ds(pl.multiple_of(lrs[k] * 128, 128), 128)])
                rhs.append(jnp.concatenate([w[left[k]], w[right[k]]], axis=1))
            at = pl.multiple_of(ccol[c] * 256, 256)
            acc[:, pl.ds(at, 256)] += jnp.dot(
                jnp.concatenate(lhs, axis=1), jnp.concatenate(rhs, axis=0), preferred_element_type=F32
            )

    for k in range(4):
        ob[k] = acc[:, k * 512 : (k + 1) * 512].astype(BF16)
        pltpu.make_async_copy(ob.at[k], out_hbm.at[k], osem.at[k]).start()
    for k in range(4):
        pltpu.make_async_copy(ob.at[k], out_hbm.at[k], osem.at[k]).wait()


def front(trow, tcol, f, tiles):
    smem = pl.BlockSpec(memory_space=pltpu.SMEM)
    hbm = pl.BlockSpec(memory_space=pl.ANY)
    listed = pltpu.SMEM((CHUNKS * GROUP,), I32)
    return pl.pallas_call(
        front_kernel,
        out_shape=jax.ShapeDtypeStruct((4, ROWS, 512), BF16),
        in_specs=[smem, smem, hbm, hbm],
        out_specs=hbm,
        scratch_shapes=[
            pltpu.VMEM((ROWS, 6144), BF16),
            pltpu.VMEM((TILES + 1, 128, 128), BF16),
            pltpu.VMEM((ROWS, 2048), F32),
            pltpu.VMEM((4, ROWS, 512), BF16),
            pltpu.SMEM((PAIRS * 96,), I32),
            listed, listed, listed,
            pltpu.SMEM((CHUNKS,), I32),
            pltpu.SemaphoreType.DMA,
            pltpu.SemaphoreType.DMA,
            pltpu.SemaphoreType.DMA((4,)),
        ],
        compiler_params=pltpu.CompilerParams(vmem_limit_bytes=VMEM),
        cost_estimate=pl.CostEstimate(flops=20 << 30, bytes_accessed=60 << 20, transcendentals=0),
        name="front",
    )(trow, tcol, f, tiles)


def route_kernel(
    smap, part, bem, out, own, x, o, of, r, req, reqin, table, high, low, slotcol, cv, perm, sm, rb,
    os, ps, pr, rs, rr, sends, recvs,
):
    me, col = lax.axis_index("row"), lax.axis_index("col")
    q, lo = col % 2, col // 2
    barrier = pltpu.get_barrier_semaphore()

    def tell(a, b):
        pl.semaphore_signal(barrier, inc=1, device_id=(a, b), device_id_type=MESH)

    tell(me, lo * 2 + 1 - q)
    tell(me, (1 - lo) * 2 + q)

    @pl.loop(1, N_ROW)
    def _(p):
        for l in range(2):
            tell(lax.rem(me + p, N_ROW), l * 2 + q)

    mine = [pltpu.make_async_copy(part.at[l * 2 + q], own.at[l], os.at[l]) for l in range(2)]
    for copy in mine:
        copy.start()
    want = jnp.concatenate([smap[0:1, :], smap[1:2, :]], axis=1)
    owner = jnp.zeros_like(want)
    for k in range(1, N_ROW):
        owner += (want >= k * ROWS).astype(I32)
    local = want - owner * ROWS
    wide = want.shape[1]

    @pl.loop(0, wide // 64)
    def _(b):
        at = pl.ds(pl.multiple_of(b * 64, 64), 64)
        here = lax.broadcasted_iota(I32, (64, wide), 0) + b * 64
        lane = lax.broadcasted_iota(I32, (64, wide), 1)
        all_owner = jnp.broadcast_to(owner, (64, wide))
        own_col = jnp.sum(jnp.where(here == lane, all_owner, 0), axis=1, keepdims=True)
        value = jnp.sum(jnp.where(here == lane, jnp.broadcast_to(local, (64, wide)), 0), axis=1, keepdims=True) + 1
        before = jnp.where((own_col == all_owner) & (lane < here), 1, 0)
        rank = jnp.sum(before, axis=1, keepdims=True)
        slotcol[at, :] = jnp.broadcast_to(own_col * CAP + rank, (64, 128))
        hit = rank == lax.broadcasted_iota(I32, (64, 128), 1)
        high[at, :] = jnp.where(hit, value >> 5, 0).astype(F32).astype(BF16)
        low[at, :] = jnp.where(hit, value & 31, 0).astype(F32).astype(BF16)

    of_source = (jnp.broadcast_to(owner, (N_ROW, wide)) == lax.broadcasted_iota(I32, (N_ROW, wide), 0))
    of_source = of_source.astype(F32).astype(BF16)
    table[...] = (
        32.0 * jnp.dot(of_source, high[...], preferred_element_type=F32)
        + jnp.dot(of_source, low[...], preferred_element_type=F32)
    ).astype(I32) - 1

    @pl.loop(0, N_ROW)
    def _(s):
        req[s] = table[pl.ds(s, 1), :]

    pl.semaphore_wait(barrier, 64)

    def swap(l):
        return pltpu.make_async_remote_copy(
            part.at[l * 2 + 1 - q], x.at[l], ps.at[l], pr.at[l], device_id=(me, lo * 2 + 1 - q), device_id_type=MESH
        )

    def ask(s, who):
        return pltpu.make_async_remote_copy(
            req.at[s], reqin.at[who], rs.at[s], rr.at[who], device_id=(s, col), device_id_type=MESH
        )

    def give(l, d, who, wl):
        return pltpu.make_async_remote_copy(
            o.at[l, d], r.at[wl, who], sends.at[l, d], recvs.at[wl, who],
            device_id=(d, l * 2 + q), device_id_type=MESH,
        )

    swap(0).start()
    swap(1).start()

    @pl.loop(1, N_ROW)
    def _(p):
        ask(lax.rem(me + p, N_ROW), me).start()

    reqin[me] = req[me]
    for l in range(2):
        mine[l].wait()
        swap(l).wait_recv()
        sm[l] = (own[l].astype(F32) + x[l].astype(F32)).astype(BF16)

    @pl.loop(1, N_ROW)
    def _(p):
        s = lax.rem(me + p, N_ROW)
        ask(s, s).wait_recv()

    lane = lax.broadcasted_iota(I32, (CAP, 128), 1)
    line = lax.broadcasted_iota(I32, (CAP, 128), 0)

    @pl.loop(0, N_ROW)
    def _(d):
        row = jnp.broadcast_to(reqin[d], (CAP, 128))
        val = jnp.sum(jnp.where(lane == line, row, 0), axis=1, keepdims=True)
        cv[pl.ds(pl.multiple_of(d * CAP, 8), CAP), :] = jnp.broadcast_to(val, (CAP, 128))

    @pl.loop(0, SLOTS // 128)
    def _(b):
        at = pl.ds(pl.multiple_of(b * 128, 128), 128)
        want = cv[at, :]
        for j in range(ROWS // 128):
            here = lax.broadcasted_iota(I32, (128, 128), 1) + j * 128
            perm[at, j * 128 : (j + 1) * 128] = (want == here).astype(F32).astype(BF16)

    for l in range(2):
        of[...] = jnp.dot(perm[...], sm[l], preferred_element_type=F32)

        @pl.loop(0, N_ROW)
        def _(d):
            o[l, d] = of[pl.ds(pl.multiple_of(d * CAP, 8), CAP), :].astype(BF16)

        @pl.loop(1, N_ROW)
        def _(p):
            give(l, lax.rem(me + p, N_ROW), me, lo).start()

    give(1 - lo, me, me, lo).start()
    r[lo, me] = o[lo, me]
    give(lo, me, me, 1 - lo).wait_recv()
    of[pl.ds(pl.multiple_of(me * CAP, 8), CAP), :] = r[0, me].astype(F32) + r[1, me].astype(F32)

    @pl.loop(1, N_ROW)
    def _(p):
        s = lax.rem(me + N_ROW - p, N_ROW)
        for l in range(2):
            give(lo, s, s, l).wait_recv()
        of[pl.ds(pl.multiple_of(s * CAP, 8), CAP), :] = r[0, s].astype(F32) + r[1, s].astype(F32)

    rb[...] = of[...].astype(BF16)
    for p in range(2):
        pick = slotcol[p * 256 : (p + 1) * 256, :]
        sel = jnp.concatenate(
            [
                (pick == lax.broadcasted_iota(I32, (256, 128), 1) + j * 128).astype(F32).astype(BF16)
                for j in range(SLOTS // 128)
            ],
            axis=1,
        )
        schur = jnp.dot(sel, rb[...], preferred_element_type=F32)
        out[p] = (bem[p].astype(F32) - schur).astype(BF16)

    for l in range(2):
        swap(l).wait_send()
    give(1 - lo, me, me, lo).wait_send()

    @pl.loop(1, N_ROW)
    def _(p):
        d = lax.rem(me + p, N_ROW)
        ask(d, me).wait_send()
        for l in range(2):
            give(l, d, me, lo).wait_send()


def route(smap, part, bem):
    hbm = pl.BlockSpec(memory_space=pl.ANY)
    vm = pl.BlockSpec(memory_space=pltpu.VMEM)
    dma = pltpu.SemaphoreType.DMA
    return pl.pallas_call(
        route_kernel,
        out_shape=jax.ShapeDtypeStruct((2, 256, 512), BF16),
        in_specs=[vm, hbm, vm],
        out_specs=vm,
        scratch_shapes=[
            pltpu.VMEM((2, ROWS, 512), BF16),
            pltpu.VMEM((2, ROWS, 512), BF16),
            pltpu.VMEM((2, N_ROW, CAP, 512), BF16),
            pltpu.VMEM((SLOTS, 512), F32),
            pltpu.VMEM((2, N_ROW, CAP, 512), BF16),
            pltpu.VMEM((N_ROW, 1, 128), I32),
            pltpu.VMEM((N_ROW, 1, 128), I32),
            pltpu.VMEM((N_ROW, 128), I32),
            pltpu.VMEM((512, 128), BF16),
            pltpu.VMEM((512, 128), BF16),
            pltpu.VMEM((512, 128), I32),
            pltpu.VMEM((SLOTS, 128), I32),
            pltpu.VMEM((SLOTS, ROWS), BF16),
            pltpu.VMEM((2, ROWS, 512), BF16),
            pltpu.VMEM((SLOTS, 512), BF16),
            dma((2,)), dma((2,)), dma((2,)), dma((N_ROW,)), dma((N_ROW,)), dma((2, N_ROW)), dma((2, N_ROW)),
        ],
        compiler_params=pltpu.CompilerParams(collective_id=0, has_side_effects=True, vmem_limit_bytes=VMEM),
        cost_estimate=pl.CostEstimate(flops=8 << 30, bytes_accessed=60 << 20, transcendentals=0),
        name="route",
    )(smap, part, bem)


def pack_kernel(j, a_piv, a_low, out, buf, isem, osem):
    me, col = lax.axis_index("row"), lax.axis_index("col")
    y, x, q = me // 8, (me // 2) % 4, col % 2
    ins = []
    for n, src in enumerate((a_piv, a_low)):
        for i in range(4):
            at = (1 - q) * (i * 4 + (x + j) % 4) + q * ((y + j) % 4 * 4 + i)
            ins.append(
                pltpu.make_async_copy(
                    src.at[:, pl.ds(pl.multiple_of(at * 512, 512), 512)], buf.at[n, i], isem.at[n, i]
                )
            )
            ins[-1].start()
    outs = []
    for n in range(2):
        for i in range(4):
            ins[n * 4 + i].wait()
            outs.append(pltpu.make_async_copy(buf.at[n, i], out.at[n, i], osem.at[n, i]))
            outs[-1].start()
    for copy in outs:
        copy.wait()


def pack(j, a_piv, a_low):
    hbm = pl.BlockSpec(memory_space=pl.ANY)
    return pl.pallas_call(
        functools.partial(pack_kernel, j),
        out_shape=jax.ShapeDtypeStruct((2, 4, 256, 512), BF16),
        in_specs=[hbm] * 2,
        out_specs=hbm,
        scratch_shapes=[
            pltpu.VMEM((2, 4, 256, 512), BF16),
            pltpu.SemaphoreType.DMA((2, 4)),
            pltpu.SemaphoreType.DMA((2, 4)),
        ],
        compiler_params=pltpu.CompilerParams(vmem_limit_bytes=VMEM),
        cost_estimate=pl.CostEstimate(flops=0, bytes_accessed=4 << 20, transcendentals=0),
        name="pack",
    )(a_piv, a_low)


def start_kernel(a_piv, a_low, half, full, buf, isem, osem):
    me, col = lax.axis_index("row"), lax.axis_index("col")
    y, x, q, lo = me // 8, (me // 2) % 4, col % 2, col // 2
    ins, outs = [], []
    for n in range(6):
        src, dst, i = (a_piv, half.at[n], 2 * lo + n) if n < 2 else (a_low, full.at[n - 2], n - 2)
        at = (1 - q) * (i * 4 + (x + 2) % 4) + q * ((y + 2) % 4 * 4 + i)
        ins.append(
            pltpu.make_async_copy(
                src.at[:, pl.ds(pl.multiple_of(at * 512, 512), 512)], buf.at[n], isem.at[n]
            )
        )
        outs.append(pltpu.make_async_copy(buf.at[n], dst, osem.at[n]))
        ins[-1].start()
    for n in range(6):
        ins[n].wait()
        outs[n].start()
    for copy in outs:
        copy.wait()


def start(a_piv, a_low):
    hbm = pl.BlockSpec(memory_space=pl.ANY)
    return pl.pallas_call(
        start_kernel,
        out_shape=[jax.ShapeDtypeStruct((n, 256, 512), BF16) for n in (2, 4)],
        in_specs=[hbm] * 2,
        out_specs=[hbm] * 2,
        scratch_shapes=[
            pltpu.VMEM((6, 256, 512), BF16),
            pltpu.SemaphoreType.DMA((6,)),
            pltpu.SemaphoreType.DMA((6,)),
        ],
        compiler_params=pltpu.CompilerParams(vmem_limit_bytes=VMEM),
        cost_estimate=pl.CostEstimate(flops=0, bytes_accessed=3 << 20, transcendentals=0),
        name="start",
    )(a_piv, a_low)


def shift(v, j):
    pairs = []
    for r in range(N_ROW):
        y, x, z = r // 8, r // 2 % 4, r % 2
        for c in range(4):
            to = (y * 4 + (x + j) % 4) * 2 + z if c % 2 == 0 else ((y + j) % 4 * 4 + x) * 2 + z
            pairs.append((r * 4 + c, to * 4 + c))
    return lax.ppermute(v, ("row", "col"), pairs)


def panel_kernel(
    asm, a_piv, a_low, m1, m2, m3, half, twin, out, tiles, b, acc, give, got,
    asem, zs, zr, gs, gr, fs, fr, ss, sr,
):
    me, col = lax.axis_index("row"), lax.axis_index("col")
    y, x, z, q = me // 8, (me // 2) % 4, me % 2, col % 2
    along = (1 - q) * y + q * x

    def on_gather(d):
        return (((y + (1 - q) * d) % 4) * 4 + (x + q * d) % 4) * 2 + z

    def on_scatter(d):
        return (((y + q * d) % 4) * 4 + (x + (1 - q) * d) % 4) * 2 + z

    other = me + 1 - 2 * z
    barrier = pltpu.get_barrier_semaphore()
    peers = [other] + [on_gather(d) for d in (1, 3, 2)] + [on_scatter(d) for d in (1, 3, 2)]
    for peer in peers:
        pl.semaphore_signal(barrier, inc=1, device_id=(peer, col), device_id_type=MESH)
    loads = []
    for n, own in enumerate((a_piv, a_low)):
        mine = []
        for i in range(4):
            at = (1 - q) * (i * 4 + x) + q * (y * 4 + i)
            mine.append(
                pltpu.make_async_copy(
                    own.at[:, pl.ds(pl.multiple_of(at * 512, 512), 512)], tiles.at[n, 0, i], asem.at[n, i]
                )
            )
        for j, src in ((1, m1), (3, m3)):
            mine.append(pltpu.make_async_copy(src.at[n], tiles.at[n, j], asem.at[n, 3 + j]))
        if n == 0:
            for k, src, which in ((5, half, col // 2), (7, twin, 1 - col // 2)):
                mine.append(pltpu.make_async_copy(src, tiles.at[n, 2, pl.ds(2 * which, 2)], asem.at[n, k]))
        else:
            mine.append(pltpu.make_async_copy(m2, tiles.at[n, 2], asem.at[n, 5]))
        for load in mine:
            load.start()
        loads.append(mine)

    sent = []

    def send(src, dst, s, r, to):
        copy = pltpu.make_async_remote_copy(src, dst, s, r, device_id=(to, col), device_id_type=MESH)
        copy.start()
        sent.append(copy)

    def hold(ref, s, r):
        pltpu.make_async_remote_copy(ref, ref, s, r, device_id=(other, col), device_id_type=MESH).wait_recv()

    def spot(d, dz):
        return (along + d) % 4 * 2 + (z + dz) % 2

    def first(n, h):
        ref = b.at[n, h, spot(0, 0)]
        send(ref, ref, zs.at[n, h], zr.at[n, h], other)
        for d in (1, 3, 2):
            send(ref, ref, gs.at[n, h, d], gr.at[n, h, d], on_gather(d))

    def relay(n, h):
        ref = b.at[n, h, spot(0, 1)]
        hold(ref, zs.at[n, h], zr.at[n, h])
        for d in (1, 3):
            send(ref, ref, fs.at[n, h, d], fr.at[n, h, d], on_gather(d))

    def near(n, h, d):
        ref = b.at[n, h, spot(d, 0)]
        hold(ref, gs.at[n, h, 4 - d], gr.at[n, h, 4 - d])
        if d == 2:
            send(ref, ref, fs.at[n, h, 2], fr.at[n, h, 2], other)

    def far(n, h, d):
        hold(b.at[n, h, spot(d, 1)], fs.at[n, h, 4 - d], fr.at[n, h, 4 - d])

    def piece(n, h, j, blocks):
        lhs = [
            tiles[n, j, (along + d) % 4, :, pl.ds(pl.multiple_of((z + dz) % 2 * 256, 256), 256)] for d, dz in blocks
        ]
        rhs = [b[n, h, spot(d, dz)] for d, dz in blocks]
        return jnp.dot(jnp.concatenate(lhs, axis=1), jnp.concatenate(rhs, axis=0), preferred_element_type=F32)

    def begin(n, h, *blocks):
        for j in range(4):
            acc[h, j] = piece(n, h, j, blocks)

    def add(n, h, *blocks):
        for j in range(4):
            acc[h, j] += piece(n, h, j, blocks)

    def last(n, h, *blocks):
        for j in (2, 1, 3):
            give[n, h, j] = (acc[h, j] + piece(n, h, j, blocks)).astype(BF16)
            send(give.at[n, h, j], got.at[n, h, j], ss.at[n, h, j], sr.at[n, h, j], on_scatter(4 - j))
        acc[h, 0] += piece(n, h, 0, blocks)

    def total(n, h):
        for j in (1, 3, 2):
            hold(got.at[n, h, j], ss.at[n, h, j], sr.at[n, h, j])
        return acc[h, 0] + (got[n, h, 1].astype(F32) + got[n, h, 3].astype(F32) + got[n, h, 2].astype(F32))

    def product(n):
        for load in loads[n]:
            load.wait()
        for h in range(2):
            near(n, h, 3)
            relay(n, h)
            near(n, h, 2)
            begin(n, h, (0, 0), (3, 0))
            near(n, h, 1)
            add(n, h, (0, 1), (1, 0))
        for h in range(2):
            far(n, h, 3)
            add(n, h, (2, 0), (3, 1))
            far(n, h, 1)
            far(n, h, 2)
            last(n, h, (1, 1), (2, 1))

    halves = [slice(h * 256, h * 256 + 256) for h in range(2)]
    for h in range(2):
        b[0, h, spot(0, 0)] = asm[0, :, halves[h]]
    pl.semaphore_wait(barrier, 7)
    for h in range(2):
        first(0, h)
    product(0)
    for h in range(2):
        solved = total(0, h).astype(BF16)
        b[1, h, spot(0, 0)] = solved
        first(1, h)
        out[0, :, halves[h]] = solved
    product(1)
    for h in range(2):
        out[1, :, halves[h]] = (asm[1, :, halves[h]].astype(F32) - total(1, h)).astype(BF16)
    for copy in sent:
        copy.wait_send()


def panel(asm, a_piv, a_low, moved):
    vm = pl.BlockSpec(memory_space=pltpu.VMEM)
    hbm = pl.BlockSpec(memory_space=pl.ANY)
    dma = pltpu.SemaphoreType.DMA
    return pl.pallas_call(
        panel_kernel,
        out_shape=jax.ShapeDtypeStruct((2, 256, 512), BF16),
        in_specs=[vm] + [hbm] * 7,
        out_specs=vm,
        scratch_shapes=[
            pltpu.VMEM((2, 4, 4, 256, 512), BF16),
            pltpu.VMEM((2, 2, 8, 256, 256), BF16),
            pltpu.VMEM((2, 4, 256, 256), F32),
            pltpu.VMEM((2, 2, 4, 256, 256), BF16),
            pltpu.VMEM((2, 2, 4, 256, 256), BF16),
            dma((2, 8)), dma((2, 2)), dma((2, 2)), dma((2, 2, 4)), dma((2, 2, 4)), dma((2, 2, 4)), dma((2, 2, 4)),
            dma((2, 2, 4)), dma((2, 2, 4)),
        ],
        compiler_params=pltpu.CompilerParams(collective_id=1, has_side_effects=True, vmem_limit_bytes=VMEM),
        cost_estimate=pl.CostEstimate(flops=4 << 30, bytes_accessed=64 << 20, transcendentals=0),
        name="panel",
    )(asm, a_piv, a_low, *moved)


def per_device(front_inverse, tiles, tile_row, tile_col, surface_map, bem, pivot, below):
    half, m2 = start(pivot, below)
    half, m2 = shift(half, 2), shift(m2, 2)
    m1 = shift(pack(1, pivot, below), 1)
    m3 = shift(pack(3, pivot, below), 3)
    part = front(tile_row, tile_col, front_inverse, tiles)
    half, part = lax.optimization_barrier((half, part))
    twin = lax.ppermute(half, "col", [(c, (c + 2) % 4) for c in range(4)])
    asm = route(surface_map, part, bem)
    return panel(asm, pivot, below, (m1, m2, m3, half, twin))


def solution(mesh):
    placed = (
        P("row", "col"),
        P("col", None, None),
        P("col"),
        P("col"),
        P(None, "row"),
        P(None, "row", "col"),
        P("row", None),
        P("row", None),
    )
    return jax.shard_map(
        per_device, mesh=mesh, in_specs=placed, out_specs=P(None, "row", "col"), check_vma=False
    )
```

```python
import jax
import jax.numpy as jnp
from jax import lax
from jax.experimental import pallas as pl
from jax.experimental.pallas import tpu as pltpu
from jax.sharding import PartitionSpec as P

MESH = pl.DeviceIdType.MESH
F32, BF16, I32 = jnp.float32, jnp.bfloat16, jnp.int32
N_ROW, CAP = 32, 24
SLOTS = N_ROW * CAP
ROWS = 768
GROUP = 4
TILES = 192
PAIRS = 8
UNROLL = 5
CHUNKS = (TILES + PAIRS * (GROUP - 1)) // GROUP + UNROLL
VMEM = 63 << 20


def front_kernel(trow, tcol, f_hbm, t_hbm, out_hbm, f, w, acc, ob, cell, left, right, lrs, ccol, fsem, tsem, osem):
    loads = [
        pltpu.make_async_copy(t_hbm, w.at[pl.ds(0, TILES)], tsem),
        pltpu.make_async_copy(f_hbm, f, fsem),
    ]
    for load in loads:
        load.start()
    first = lax.axis_index("col") * 48

    @pl.loop(0, PAIRS * 12)
    def _(i):
        for u in range(8):
            cell[i * 8 + u] = TILES

    def fill(i, _):
        b = tcol[i]
        cell[(b // 2) * 96 + (trow[i] - first) * 2 + b % 2] = i
        return 0

    lax.fori_loop(0, TILES, fill, 0, unroll=8)

    def finish(n):
        for g in range(GROUP):
            left[n + g] = TILES
            right[n + g] = TILES
            lrs[n + g] = 0
        return (n + GROUP - 1) // GROUP * GROUP

    def place(b, n):
        def visit(lr, n):
            one, two = cell[b * 96 + lr * 2], cell[b * 96 + lr * 2 + 1]
            left[n], right[n], lrs[n] = one, two, lr
            return n + jnp.where(one + two == 2 * TILES, 0, 1)

        end = finish(lax.fori_loop(0, 48, visit, n, unroll=4))

        def name(c, _):
            ccol[c] = b
            return 0

        lax.fori_loop(n // GROUP, end // GROUP, name, 0)
        return end

    total = lax.fori_loop(0, PAIRS, place, 0) // GROUP
    for u in range(UNROLL - 1):
        finish((total + u) * GROUP)
        ccol[total + u] = 0
    w[TILES] = jnp.zeros((128, 128), BF16)
    acc[...] = jnp.zeros_like(acc)
    for load in loads:
        load.wait()

    @pl.loop(0, (total + UNROLL - 1) // UNROLL)
    def _(it):
        for u in range(UNROLL):
            c = it * UNROLL + u
            lhs, rhs = [], []
            for g in range(GROUP):
                k = c * GROUP + g
                lhs.append(f[:, pl.ds(pl.multiple_of(lrs[k] * 128, 128), 128)])
                rhs.append(jnp.concatenate([w[left[k]], w[right[k]]], axis=1))
            at = pl.multiple_of(ccol[c] * 256, 256)
            acc[:, pl.ds(at, 256)] += jnp.dot(
                jnp.concatenate(lhs, axis=1), jnp.concatenate(rhs, axis=0), preferred_element_type=F32
            )

    for k in range(4):
        ob[k] = acc[:, k * 512 : (k + 1) * 512].astype(BF16)
        pltpu.make_async_copy(ob.at[k], out_hbm.at[k], osem.at[k]).start()
    for k in range(4):
        pltpu.make_async_copy(ob.at[k], out_hbm.at[k], osem.at[k]).wait()


def front(trow, tcol, f, tiles):
    smem = pl.BlockSpec(memory_space=pltpu.SMEM)
    hbm = pl.BlockSpec(memory_space=pl.ANY)
    listed = pltpu.SMEM((CHUNKS * GROUP,), I32)
    return pl.pallas_call(
        front_kernel,
        out_shape=jax.ShapeDtypeStruct((4, ROWS, 512), BF16),
        in_specs=[smem, smem, hbm, hbm],
        out_specs=hbm,
        scratch_shapes=[
            pltpu.VMEM((ROWS, 6144), BF16),
            pltpu.VMEM((TILES + 1, 128, 128), BF16),
            pltpu.VMEM((ROWS, 2048), F32),
            pltpu.VMEM((4, ROWS, 512), BF16),
            pltpu.SMEM((PAIRS * 96,), I32),
            listed, listed, listed,
            pltpu.SMEM((CHUNKS,), I32),
            pltpu.SemaphoreType.DMA,
            pltpu.SemaphoreType.DMA,
            pltpu.SemaphoreType.DMA((4,)),
        ],
        compiler_params=pltpu.CompilerParams(vmem_limit_bytes=VMEM),
        cost_estimate=pl.CostEstimate(flops=20 << 30, bytes_accessed=60 << 20, transcendentals=0),
        name="front",
    )(trow, tcol, f, tiles)


def route_kernel(
    smap, part, bem, out, own, x, o, of, r, req, reqin, table, high, low, slotcol, cv, perm, sm, rb,
    os, ps, pr, rs, rr, sends, recvs,
):
    me, col = lax.axis_index("row"), lax.axis_index("col")
    q, lo = col % 2, col // 2
    barrier = pltpu.get_barrier_semaphore()

    def tell(a, b):
        pl.semaphore_signal(barrier, inc=1, device_id=(a, b), device_id_type=MESH)

    tell(me, lo * 2 + 1 - q)
    tell(me, (1 - lo) * 2 + q)

    @pl.loop(1, N_ROW)
    def _(p):
        for l in range(2):
            tell(lax.rem(me + p, N_ROW), l * 2 + q)

    mine = [pltpu.make_async_copy(part.at[l * 2 + q], own.at[l], os.at[l]) for l in range(2)]
    for copy in mine:
        copy.start()
    want = jnp.concatenate([smap[0:1, :], smap[1:2, :]], axis=1)
    owner = jnp.zeros_like(want)
    for k in range(1, N_ROW):
        owner += (want >= k * ROWS).astype(I32)
    local = want - owner * ROWS
    wide = want.shape[1]

    @pl.loop(0, wide // 64)
    def _(b):
        at = pl.ds(pl.multiple_of(b * 64, 64), 64)
        here = lax.broadcasted_iota(I32, (64, wide), 0) + b * 64
        lane = lax.broadcasted_iota(I32, (64, wide), 1)
        all_owner = jnp.broadcast_to(owner, (64, wide))
        own_col = jnp.sum(jnp.where(here == lane, all_owner, 0), axis=1, keepdims=True)
        value = jnp.sum(jnp.where(here == lane, jnp.broadcast_to(local, (64, wide)), 0), axis=1, keepdims=True) + 1
        before = jnp.where((own_col == all_owner) & (lane < here), 1, 0)
        rank = jnp.sum(before, axis=1, keepdims=True)
        slotcol[at, :] = jnp.broadcast_to(own_col * CAP + rank, (64, 128))
        hit = rank == lax.broadcasted_iota(I32, (64, 128), 1)
        high[at, :] = jnp.where(hit, value >> 5, 0).astype(F32).astype(BF16)
        low[at, :] = jnp.where(hit, value & 31, 0).astype(F32).astype(BF16)

    of_source = (jnp.broadcast_to(owner, (N_ROW, wide)) == lax.broadcasted_iota(I32, (N_ROW, wide), 0))
    of_source = of_source.astype(F32).astype(BF16)
    table[...] = (
        32.0 * jnp.dot(of_source, high[...], preferred_element_type=F32)
        + jnp.dot(of_source, low[...], preferred_element_type=F32)
    ).astype(I32) - 1

    @pl.loop(0, N_ROW)
    def _(s):
        req[s] = table[pl.ds(s, 1), :]

    pl.semaphore_wait(barrier, 64)

    def swap(l):
        return pltpu.make_async_remote_copy(
            part.at[l * 2 + 1 - q], x.at[l], ps.at[l], pr.at[l], device_id=(me, lo * 2 + 1 - q), device_id_type=MESH
        )

    def ask(s, who):
        return pltpu.make_async_remote_copy(
            req.at[s], reqin.at[who], rs.at[s], rr.at[who], device_id=(s, col), device_id_type=MESH
        )

    def give(l, d, who, wl):
        return pltpu.make_async_remote_copy(
            o.at[l, d], r.at[wl, who], sends.at[l, d], recvs.at[wl, who],
            device_id=(d, l * 2 + q), device_id_type=MESH,
        )

    swap(0).start()
    swap(1).start()

    @pl.loop(1, N_ROW)
    def _(p):
        ask(lax.rem(me + p, N_ROW), me).start()

    reqin[me] = req[me]
    for l in range(2):
        mine[l].wait()
        swap(l).wait_recv()
        sm[l] = (own[l].astype(F32) + x[l].astype(F32)).astype(BF16)

    @pl.loop(1, N_ROW)
    def _(p):
        s = lax.rem(me + p, N_ROW)
        ask(s, s).wait_recv()

    lane = lax.broadcasted_iota(I32, (CAP, 128), 1)
    line = lax.broadcasted_iota(I32, (CAP, 128), 0)

    @pl.loop(0, N_ROW)
    def _(d):
        row = jnp.broadcast_to(reqin[d], (CAP, 128))
        val = jnp.sum(jnp.where(lane == line, row, 0), axis=1, keepdims=True)
        cv[pl.ds(pl.multiple_of(d * CAP, 8), CAP), :] = jnp.broadcast_to(val, (CAP, 128))

    @pl.loop(0, SLOTS // 128)
    def _(b):
        at = pl.ds(pl.multiple_of(b * 128, 128), 128)
        want = cv[at, :]
        for j in range(ROWS // 128):
            here = lax.broadcasted_iota(I32, (128, 128), 1) + j * 128
            perm[at, j * 128 : (j + 1) * 128] = (want == here).astype(F32).astype(BF16)

    for l in range(2):
        of[...] = jnp.dot(perm[...], sm[l], preferred_element_type=F32)

        @pl.loop(0, N_ROW)
        def _(d):
            o[l, d] = of[pl.ds(pl.multiple_of(d * CAP, 8), CAP), :].astype(BF16)

        @pl.loop(1, N_ROW)
        def _(p):
            give(l, lax.rem(me + p, N_ROW), me, lo).start()

    give(1 - lo, me, me, lo).start()
    r[lo, me] = o[lo, me]
    give(lo, me, me, 1 - lo).wait_recv()
    of[pl.ds(pl.multiple_of(me * CAP, 8), CAP), :] = r[0, me].astype(F32) + r[1, me].astype(F32)

    @pl.loop(1, N_ROW)
    def _(p):
        s = lax.rem(me + N_ROW - p, N_ROW)
        for l in range(2):
            give(lo, s, s, l).wait_recv()
        of[pl.ds(pl.multiple_of(s * CAP, 8), CAP), :] = r[0, s].astype(F32) + r[1, s].astype(F32)

    rb[...] = of[...].astype(BF16)
    for p in range(2):
        pick = slotcol[p * 256 : (p + 1) * 256, :]
        sel = jnp.concatenate(
            [
                (pick == lax.broadcasted_iota(I32, (256, 128), 1) + j * 128).astype(F32).astype(BF16)
                for j in range(SLOTS // 128)
            ],
            axis=1,
        )
        schur = jnp.dot(sel, rb[...], preferred_element_type=F32)
        out[p] = (bem[p].astype(F32) - schur).astype(BF16)

    for l in range(2):
        swap(l).wait_send()
    give(1 - lo, me, me, lo).wait_send()

    @pl.loop(1, N_ROW)
    def _(p):
        d = lax.rem(me + p, N_ROW)
        ask(d, me).wait_send()
        for l in range(2):
            give(l, d, me, lo).wait_send()


def route(smap, part, bem):
    hbm = pl.BlockSpec(memory_space=pl.ANY)
    vm = pl.BlockSpec(memory_space=pltpu.VMEM)
    dma = pltpu.SemaphoreType.DMA
    return pl.pallas_call(
        route_kernel,
        out_shape=jax.ShapeDtypeStruct((2, 256, 512), BF16),
        in_specs=[vm, hbm, vm],
        out_specs=vm,
        scratch_shapes=[
            pltpu.VMEM((2, ROWS, 512), BF16),
            pltpu.VMEM((2, ROWS, 512), BF16),
            pltpu.VMEM((2, N_ROW, CAP, 512), BF16),
            pltpu.VMEM((SLOTS, 512), F32),
            pltpu.VMEM((2, N_ROW, CAP, 512), BF16),
            pltpu.VMEM((N_ROW, 1, 128), I32),
            pltpu.VMEM((N_ROW, 1, 128), I32),
            pltpu.VMEM((N_ROW, 128), I32),
            pltpu.VMEM((512, 128), BF16),
            pltpu.VMEM((512, 128), BF16),
            pltpu.VMEM((512, 128), I32),
            pltpu.VMEM((SLOTS, 128), I32),
            pltpu.VMEM((SLOTS, ROWS), BF16),
            pltpu.VMEM((2, ROWS, 512), BF16),
            pltpu.VMEM((SLOTS, 512), BF16),
            dma((2,)), dma((2,)), dma((2,)), dma((N_ROW,)), dma((N_ROW,)), dma((2, N_ROW)), dma((2, N_ROW)),
        ],
        compiler_params=pltpu.CompilerParams(collective_id=0, has_side_effects=True, vmem_limit_bytes=VMEM),
        cost_estimate=pl.CostEstimate(flops=8 << 30, bytes_accessed=60 << 20, transcendentals=0),
        name="route",
    )(smap, part, bem)


def start_kernel(a_piv, a_low, half, m1, m2, m3, buf, isem, osem):
    me, col = lax.axis_index("row"), lax.axis_index("col")
    y, x, q, lo = me // 8, (me // 2) % 4, col % 2, col // 2
    moves = [(2, a_piv, half.at[n], 2 * lo + n) for n in range(2)]
    for j, dst in ((1, m1), (3, m3)):
        for n, src in enumerate((a_piv, a_low)):
            moves += [(j, src, dst.at[n, i], i) for i in range(4)]
    moves += [(2, a_low, m2.at[i], i) for i in range(4)]
    ins, outs = [], []
    for n, (j, src, dst, i) in enumerate(moves):
        at = (1 - q) * (i * 4 + (x + j) % 4) + q * ((y + j) % 4 * 4 + i)
        ins.append(
            pltpu.make_async_copy(
                src.at[:, pl.ds(pl.multiple_of(at * 512, 512), 512)], buf.at[n], isem.at[n]
            )
        )
        outs.append(pltpu.make_async_copy(buf.at[n], dst, osem.at[n]))
        ins[-1].start()
    for arrived, leave in zip(ins, outs):
        arrived.wait()
        leave.start()
    for copy in outs:
        copy.wait()


def start(a_piv, a_low):
    hbm = pl.BlockSpec(memory_space=pl.ANY)
    return pl.pallas_call(
        start_kernel,
        out_shape=[
            jax.ShapeDtypeStruct((*n, 256, 512), BF16) for n in ((2,), (2, 4), (4,), (2, 4))
        ],
        in_specs=[hbm] * 2,
        out_specs=[hbm] * 4,
        scratch_shapes=[
            pltpu.VMEM((22, 256, 512), BF16),
            pltpu.SemaphoreType.DMA((22,)),
            pltpu.SemaphoreType.DMA((22,)),
        ],
        compiler_params=pltpu.CompilerParams(vmem_limit_bytes=VMEM),
        cost_estimate=pl.CostEstimate(flops=0, bytes_accessed=11 << 20, transcendentals=0),
        name="start",
    )(a_piv, a_low)


def shift(v, j):
    pairs = []
    for r in range(N_ROW):
        y, x, z = r // 8, r // 2 % 4, r % 2
        for c in range(4):
            to = (y * 4 + (x + j) % 4) * 2 + z if c % 2 == 0 else ((y + j) % 4 * 4 + x) * 2 + z
            pairs.append((r * 4 + c, to * 4 + c))
    return lax.ppermute(v, ("row", "col"), pairs)


def panel_kernel(
    asm, a_piv, a_low, m1, m2, m3, half, twin, out, tiles, b, acc, give, got,
    asem, zs, zr, gs, gr, fs, fr, ss, sr,
):
    me, col = lax.axis_index("row"), lax.axis_index("col")
    y, x, z, q = me // 8, (me // 2) % 4, me % 2, col % 2
    along = (1 - q) * y + q * x

    def on_gather(d):
        return (((y + (1 - q) * d) % 4) * 4 + (x + q * d) % 4) * 2 + z

    def on_scatter(d):
        return (((y + q * d) % 4) * 4 + (x + (1 - q) * d) % 4) * 2 + z

    other = me + 1 - 2 * z
    barrier = pltpu.get_barrier_semaphore()
    peers = [other] + [on_gather(d) for d in (1, 3, 2)] + [on_scatter(d) for d in (1, 3, 2)]
    for peer in peers:
        pl.semaphore_signal(barrier, inc=1, device_id=(peer, col), device_id_type=MESH)
    loads = []
    for n, own in enumerate((a_piv, a_low)):
        mine = []
        for i in range(4):
            at = (1 - q) * (i * 4 + x) + q * (y * 4 + i)
            mine.append(
                pltpu.make_async_copy(
                    own.at[:, pl.ds(pl.multiple_of(at * 512, 512), 512)], tiles.at[n, 0, i], asem.at[n, i]
                )
            )
        for j, src in ((1, m1), (3, m3)):
            mine.append(pltpu.make_async_copy(src.at[n], tiles.at[n, j], asem.at[n, 3 + j]))
        if n == 0:
            for k, src, which in ((5, half, col // 2), (7, twin, 1 - col // 2)):
                mine.append(pltpu.make_async_copy(src, tiles.at[n, 2, pl.ds(2 * which, 2)], asem.at[n, k]))
        else:
            mine.append(pltpu.make_async_copy(m2, tiles.at[n, 2], asem.at[n, 5]))
        for load in mine:
            load.start()
        loads.append(mine)

    sent = []

    def send(src, dst, s, r, to):
        copy = pltpu.make_async_remote_copy(src, dst, s, r, device_id=(to, col), device_id_type=MESH)
        copy.start()
        sent.append(copy)

    def hold(ref, s, r):
        pltpu.make_async_remote_copy(ref, ref, s, r, device_id=(other, col), device_id_type=MESH).wait_recv()

    def spot(d, dz):
        return (along + d) % 4 * 2 + (z + dz) % 2

    def first(n, h):
        ref = b.at[n, h, spot(0, 0)]
        send(ref, ref, zs.at[n, h], zr.at[n, h], other)
        for d in (1, 3, 2):
            send(ref, ref, gs.at[n, h, d], gr.at[n, h, d], on_gather(d))

    def relay(n, h):
        ref = b.at[n, h, spot(0, 1)]
        hold(ref, zs.at[n, h], zr.at[n, h])
        for d in (1, 3):
            send(ref, ref, fs.at[n, h, d], fr.at[n, h, d], on_gather(d))

    def near(n, h, d):
        ref = b.at[n, h, spot(d, 0)]
        hold(ref, gs.at[n, h, 4 - d], gr.at[n, h, 4 - d])
        if d == 2:
            send(ref, ref, fs.at[n, h, 2], fr.at[n, h, 2], other)

    def far(n, h, d):
        hold(b.at[n, h, spot(d, 1)], fs.at[n, h, 4 - d], fr.at[n, h, 4 - d])

    def piece(n, h, j, blocks):
        lhs = [
            tiles[n, j, (along + d) % 4, :, pl.ds(pl.multiple_of((z + dz) % 2 * 256, 256), 256)] for d, dz in blocks
        ]
        rhs = [b[n, h, spot(d, dz)] for d, dz in blocks]
        return jnp.dot(jnp.concatenate(lhs, axis=1), jnp.concatenate(rhs, axis=0), preferred_element_type=F32)

    def begin(n, h, *blocks):
        for j in range(4):
            acc[h, j] = piece(n, h, j, blocks)

    def add(n, h, *blocks):
        for j in range(4):
            acc[h, j] += piece(n, h, j, blocks)

    def last(n, h, *blocks):
        for j in (2, 1, 3):
            give[n, h, j] = (acc[h, j] + piece(n, h, j, blocks)).astype(BF16)
            send(give.at[n, h, j], got.at[n, h, j], ss.at[n, h, j], sr.at[n, h, j], on_scatter(4 - j))
        acc[h, 0] += piece(n, h, 0, blocks)

    def total(n, h):
        for j in (1, 3, 2):
            hold(got.at[n, h, j], ss.at[n, h, j], sr.at[n, h, j])
        return acc[h, 0] + (got[n, h, 1].astype(F32) + got[n, h, 3].astype(F32) + got[n, h, 2].astype(F32))

    def product(n):
        for load in loads[n]:
            load.wait()
        for h in range(2):
            near(n, h, 3)
            relay(n, h)
            near(n, h, 2)
            begin(n, h, (0, 0), (3, 0))
            near(n, h, 1)
            add(n, h, (0, 1), (1, 0))
        for h in range(2):
            far(n, h, 3)
            add(n, h, (2, 0), (3, 1))
            far(n, h, 1)
            far(n, h, 2)
            last(n, h, (1, 1), (2, 1))

    halves = [slice(h * 256, h * 256 + 256) for h in range(2)]
    for h in range(2):
        b[0, h, spot(0, 0)] = asm[0, :, halves[h]]
    pl.semaphore_wait(barrier, 7)
    for h in range(2):
        first(0, h)
    product(0)
    for h in range(2):
        solved = total(0, h).astype(BF16)
        b[1, h, spot(0, 0)] = solved
        first(1, h)
        out[0, :, halves[h]] = solved
    product(1)
    for h in range(2):
        out[1, :, halves[h]] = (asm[1, :, halves[h]].astype(F32) - total(1, h)).astype(BF16)
    for copy in sent:
        copy.wait_send()


def panel(asm, a_piv, a_low, moved):
    vm = pl.BlockSpec(memory_space=pltpu.VMEM)
    hbm = pl.BlockSpec(memory_space=pl.ANY)
    dma = pltpu.SemaphoreType.DMA
    return pl.pallas_call(
        panel_kernel,
        out_shape=jax.ShapeDtypeStruct((2, 256, 512), BF16),
        in_specs=[vm] + [hbm] * 7,
        out_specs=vm,
        scratch_shapes=[
            pltpu.VMEM((2, 4, 4, 256, 512), BF16),
            pltpu.VMEM((2, 2, 8, 256, 256), BF16),
            pltpu.VMEM((2, 4, 256, 256), F32),
            pltpu.VMEM((2, 2, 4, 256, 256), BF16),
            pltpu.VMEM((2, 2, 4, 256, 256), BF16),
            dma((2, 8)), dma((2, 2)), dma((2, 2)), dma((2, 2, 4)), dma((2, 2, 4)), dma((2, 2, 4)), dma((2, 2, 4)),
            dma((2, 2, 4)), dma((2, 2, 4)),
        ],
        compiler_params=pltpu.CompilerParams(collective_id=1, has_side_effects=True, vmem_limit_bytes=VMEM),
        cost_estimate=pl.CostEstimate(flops=4 << 30, bytes_accessed=64 << 20, transcendentals=0),
        name="panel",
    )(asm, a_piv, a_low, *moved)


def per_device(front_inverse, tiles, tile_row, tile_col, surface_map, bem, pivot, below):
    half, m1, m2, m3 = start(pivot, below)
    half, m1, m3, m2 = shift(half, 2), shift(m1, 1), shift(m3, 3), shift(m2, 2)
    part = front(tile_row, tile_col, front_inverse, tiles)
    half, part = lax.optimization_barrier((half, part))
    twin = lax.ppermute(half, "col", [(c, (c + 2) % 4) for c in range(4)])
    asm = route(surface_map, part, bem)
    return panel(asm, pivot, below, (m1, m2, m3, half, twin))


def solution(mesh):
    placed = (
        P("row", "col"),
        P("col", None, None),
        P("col"),
        P("col"),
        P(None, "row"),
        P(None, "row", "col"),
        P("row", None),
        P("row", None),
    )
    return jax.shard_map(
        per_device, mesh=mesh, in_specs=placed, out_specs=P(None, "row", "col"), check_vma=False
    )
```
